768 devices in a mesh: slab: 8 (over x, core), tile: 96 (over z, y).
Axes of the slice: x: 4, y: 8, z: 12, core: 2. Of those that a mesh axis runs over, the one named last changes fastest.
Arguments:
- right_side: float32 [64, 1536, 128], P('slab', 'tile'), may hold values from -8 to 8
- diagonal: float32 [64, 1536, 128], P('slab', 'tile'), may hold values from 0.25 to 2
- inlet_index: int32 [8, 96, 384, 16], P('slab', 'tile'), may hold values from 0 to 16383
- plate_order: int32 [384], replicated, may hold values from 0 to 383, each once
- conductance: float32 [384], P('tile'), may hold values from 0.5 to 2
- plate_level: float32 [384], P('tile'), may hold values from -3 to 3
Outputs:
- solution: float32 [64, 1536, 128], P('slab', 'tile')
- residual: float32 [64, 1536, 128], P('slab', 'tile')
- inlet_flow: float32 [384], P('tile')
The draws below stay inside these ranges and needn't reach their ends.
Inputs may be any that keep to these rules, and one draw needn't show every extreme that they name: `inlet_index`: each entry is a cell of the block of the device given by the first two indices. `plate_order`: each plate appears once.
All inputs are finite; a program needn't handle non-finite values.
Results may differ from the reference program's by a relative error of at most 0.0003.
Values sent between devices are 32-bit elements; how exact they have to be, the bound alone decides.
No kernel may reach another device: no remote copies, remote signals or barrier semaphores. Data moves between devices by JAX's collectives and lax.ppermute only.
A program may use at most 32 MiB of HBM per device.

```python
import math
import jax
import jax.numpy as jnp
from jax import lax

CZ = 8
CY = 16
NX = 128
STEPS = 4
BLOCKS = 2
INLETS = 16
NZ = 64
NY = 1536
PLATES = 384
N_SLAB = 8
N_TILE = 96


def set_ends(array, own_key, least, largest):
    spot = [jax.random.randint(jax.random.fold_in(own_key, axis), (), 0, length) for axis, length in enumerate(array.shape)]
    main_axis = array.shape.index(max(array.shape))
    neighbour = spot[:main_axis] + [(spot[main_axis] + 1) % array.shape[main_axis]] + spot[main_axis + 1:]
    return array.at[tuple(spot)].set(least).at[tuple(neighbour)].set(largest)


def block_scale(own_key, extent, cuts, low, high):
    level, own = 1.0, jax.random.fold_in(own_key, 6)
    for dim, shards_of in cuts:
        steps = jnp.exp(jax.random.uniform(jax.random.fold_in(own, dim), (shards_of,), jnp.float32, low / len(cuts), high / len(cuts)))
        level = level * jnp.repeat(steps, extent[dim] // shards_of).reshape([-1 if axis == dim else 1 for axis in range(len(extent))])
    return level


def scatter_about(rng, shape, spread, bound, split=(), dtype=jnp.bfloat16):
    values = jax.random.normal(rng, shape, jnp.float32) * spread
    if len(split) > 0:
        values = block_scale(rng, shape, split, -0.22, 0.18) * values
    return jnp.clip(values, min=-bound, max=bound).astype(dtype)


def setup_inputs(seed: int = 0) -> dict:
    splits = jax.random.split(jax.random.key(seed), 7)
    right_side = scatter_about(splits[0], (NZ, NY, NX), 1.0, 8.0, ((0, 8), (1, 96)), jnp.float32)
    diagonal = jnp.clip(0.25 + 1.75 * jax.random.uniform(splits[1], (NZ, NY, NX), jnp.float32) ** block_scale(splits[1], (NZ, NY, NX), ((0, 8), (1, 96)), -0.2, 0.2), 0.25, 2.0)
    inlet_index = set_ends(jax.random.randint(splits[2], (N_SLAB, N_TILE, PLATES, INLETS), 0, CZ * CY * NX), jax.random.fold_in(splits[2], 1), 0, (CZ * CY * NX) - 1).astype(jnp.int32)
    plate_order = jax.random.permutation(splits[3], PLATES).astype(jnp.int32)
    conductance = jnp.clip(jnp.exp(math.log(2.0) - 1.3862944 * jax.random.uniform(splits[4], (PLATES,), jnp.float32) ** block_scale(splits[4], (PLATES,), ((0, 96),), -0.2, 0.2)), 0.5, 2.0)
    plate_level = scatter_about(splits[5], (PLATES,), 0.5, 3.0, ((0, 96),), jnp.float32)
    return {"right_side": right_side, "diagonal": diagonal, "inlet_index": inlet_index, "plate_order": plate_order, "conductance": conductance, "plate_level": plate_level}


GRAM_PAIRS = [(row_at, col_at) for row_at in range(5) for col_at in range(row_at, 5)]

def apply_shifted(padded, diagonal):
    center = padded[1:-1, 1:-1]
    zero_col = jnp.zeros_like(center[:, :, :1])
    beside = padded[2:, 1:-1] + padded[:-2, 1:-1]
    beside = beside + padded[1:-1, 2:] + padded[1:-1, :-2]
    beside = beside + jnp.concatenate([center[:, :, 1:], zero_col], axis=2) + jnp.concatenate([zero_col, center[:, :, :-1]], axis=2)
    return ((diagonal - 1.0) * center - beside) / 7.0

def cholesky_solve(matrix, rhs):
    factor = jnp.linalg.cholesky(matrix)
    forward = []
    for row_at in range(4):
        value = rhs[row_at]
        for col_at in range(row_at):
            value = value - factor[row_at, col_at] * forward[col_at]
        forward.append(value / factor[row_at, row_at])
    backward = [None] * 4
    for row_at in range(3, -1, -1):
        value = forward[row_at]
        for col_at in range(row_at + 1, 4):
            value = value - factor[col_at, row_at] * backward[col_at]
        backward[row_at] = value / factor[row_at, row_at]
    return jnp.stack(backward)

def solve_block(gram_vec):
    entries = {}
    for place, pair in enumerate(GRAM_PAIRS):
        entries[pair] = gram_vec[place]
        entries[pair[1], pair[0]] = gram_vec[place]
    gram = jnp.stack([jnp.stack([entries[row_at, col_at] for col_at in range(5)]) for row_at in range(5)])
    matrix = 7.0 * (gram[:4, 1:] + gram[:4, :4])
    matrix = 0.5 * (matrix + matrix.T)
    return cholesky_solve(matrix, gram[:4, 0])

def update(solution, residual, basis, coeffs):
    for degree in range(4):
        solution = solution + coeffs[degree] * basis[degree]
        residual = residual - 7.0 * coeffs[degree] * (basis[degree + 1] + basis[degree])
    return (solution, residual)

def reference(right_side, diagonal, inlet_index, plate_order, conductance, plate_level):
    solution = jnp.zeros_like(right_side)
    residual = right_side
    for repeat in range(BLOCKS):
        basis = [residual]
        for degree in range(STEPS):
            padded = jnp.pad(basis[-1], ((1, 1), (1, 1), (0, 0)))
            basis.append(apply_shifted(padded, diagonal))
        gram_vec = jnp.stack([jnp.sum(basis[pair[0]] * basis[pair[1]]) for pair in GRAM_PAIRS])
        coeffs = solve_block(gram_vec)
        solution, residual = update(solution, residual, basis, coeffs)
    blocks = solution.reshape(N_SLAB, CZ, N_TILE, CY, NX).transpose(0, 2, 1, 3, 4).reshape(N_SLAB, N_TILE, CZ * CY * NX)
    picked = jnp.take_along_axis(blocks, inlet_index.reshape(N_SLAB, N_TILE, PLATES * INLETS).astype(jnp.int32), axis=2)
    contrib = lax.optimization_barrier(jnp.sum(picked.reshape(N_SLAB, N_TILE, PLATES, INLETS), axis=(0, 1, 3)))
    scale = 1.0 / jnp.sqrt(jnp.float32(N_SLAB * N_TILE * INLETS))
    header = jnp.take(contrib, plate_order, axis=0) * scale
    inlet_flow = conductance * (header - plate_level)
    return (solution, residual, inlet_flow)
```

```python
import functools

import jax
import jax.numpy as jnp
from jax import lax
from jax.experimental import pallas as pl
from jax.experimental.pallas import tpu as pltpu
from jax.sharding import PartitionSpec as P

HALO = 8
DEGREE = 8
FIELDS = 8
OWNED = 4
LANES = 128
MOMENT_LANE = 32
LOW_LANE = 64


def two_sum(a, b):
    s = a + b
    v = s - a
    return s, (a - (s - v)) + (b - v)


def quick_two_sum(a, b):
    s = a + b
    return s, b - (s - a)


def split(a):
    c = a * 4097.0
    high = c - (c - a)
    return high, a - high


def two_prod(a, b):
    p = a * b
    ah, al = split(a)
    bh, bl = split(b)
    return p, ((ah * bh - p) + ah * bl + al * bh) + al * bl


def dd_add(x, y):
    s, e = two_sum(x[0], y[0])
    t, f = two_sum(x[1], y[1])
    s, e = quick_two_sum(s, e + t)
    return quick_two_sum(s, e + f)


def dd_mul(x, y):
    p, e = two_prod(x[0], y[0])
    return quick_two_sum(p, e + (x[0] * y[1] + x[1] * y[0]))


def dd_scale(x, power):
    return x[0] * power, x[1] * power


def dd_neg(x):
    return -x[0], -x[1]


def dd_sum(terms):
    total = terms[0]
    for term in terms[1:]:
        total = dd_add(total, term)
    return total


def lane_of(shape):
    return lax.broadcasted_iota(jnp.int32, shape, len(shape) - 1)


def basis_kernel(own, low, high, index, order, payload, basis, last, alpha, beta, even, odd, parts, sums):
    cz = own.shape[1]
    wide_y = own.shape[2]
    cy = wide_y - 2 * HALO
    for place, source in enumerate((low, own, high)):
        at = pl.ds(place * cz, cz)
        even[at] = source[0]
        diag = source[1]
        inside = jnp.where(diag > 0.0, 0.25, 0.0)
        beta[at] = inside
        alpha[at] = (diag - 1.0) * inside
    lane = lane_of((wide_y, LANES))
    planes = 3 * cz

    def emit(field, degree):
        for z in range(cz):
            value = field[cz + z, HALO : HALO + cy, :]
            if degree < FIELDS:
                basis[pl.ds(z * cy * FIELDS + degree, cy, stride=FIELDS), :] = value
            else:
                last[pl.ds(z * cy, cy), :] = value

    def product(first, second, slot):
        total = None
        for z in range(cz):
            term = first[cz + z, HALO : HALO + cy, :] * second[cz + z, HALO : HALO + cy, :]
            term = term[:8] + term[8:]
            total = term if total is None else total + term
        parts[pl.ds(slot * 8, 8), :] = total

    emit(even, 0)
    product(even, even, 0)
    now, later = even, odd
    for degree in range(DEGREE):

        def plane(z, carry, now=now, later=later, degree=degree):
            value = now[z]
            beside = now[z - 1] + now[z + 1]
            beside = beside + pltpu.roll(value, 1, 0) + pltpu.roll(value, wide_y - 1, 0)
            beside = beside + jnp.where(lane == 0, 0.0, pltpu.roll(value, 1, 1))
            beside = beside + jnp.where(lane == LANES - 1, 0.0, pltpu.roll(value, LANES - 1, 1))
            fresh = alpha[z] * value - beta[z] * beside
            if degree == 0:
                later[z] = 0.5 * fresh
            else:
                later[z] = fresh - later[z]
            return carry

        lax.fori_loop(degree + 1, planes - 1 - degree, plane, 0, unroll=2)
        emit(later, degree + 1)
        product(now, later, 2 * degree + 1)
        product(later, later, 2 * degree + 2)
        now, later = later, now

    slots = parts.shape[0] // 8
    for slot in range(2 * DEGREE + 1, slots):
        parts[pl.ds(slot * 8, 8), :] = jnp.zeros((8, LANES), jnp.float32)
    value = parts[pl.ds(0, slots, stride=8), :]
    error = jnp.zeros_like(value)
    for row in range(1, 8):
        value, extra = two_sum(value, parts[pl.ds(row, slots, stride=8), :])
        error = error + extra
    step = LANES // 2
    while step:
        value, extra = two_sum(value, pltpu.roll(value, step, 1))
        error = error + pltpu.roll(error, step, 1) + extra
        step //= 2
    value, error = quick_two_sum(value, error)
    lane_s = lane_of((slots, LANES))
    row_s = lax.broadcasted_iota(jnp.int32, (slots, LANES), 0)
    placed = jnp.where(lane_s == MOMENT_LANE + row_s, value, 0.0)
    placed = placed + jnp.where(lane_s == LOW_LANE + row_s, error, 0.0)
    moments = jnp.sum(placed, axis=0, keepdims=True)

    lane_v = lane_of((FIELDS, LANES))
    inlets = index.shape[0] // order.shape[0]

    def plate(at, carry):
        start = order[at] * inlets
        total = None
        for slot in range(inlets):
            cell = index[start + slot]
            row = pl.multiple_of((cell >> 7) * FIELDS, FIELDS)
            picked = jnp.where(lane_v == (cell & 127), basis[pl.ds(row, FIELDS), :], 0.0)
            total = picked if total is None else total + picked
        sums[pl.ds(pl.multiple_of(at * FIELDS, FIELDS), FIELDS), :] = total
        return carry

    lax.fori_loop(0, order.shape[0], plate, 0, unroll=2)
    tiles = payload.shape[0]
    lane_t = lane_of((tiles, LANES))
    out = jnp.broadcast_to(moments, (tiles, LANES))
    for slot in range(OWNED * FIELDS):
        column = sums[pl.ds(slot, tiles, stride=OWNED * FIELDS), :]
        out = jnp.where(lane_t == slot, jnp.sum(column, axis=1, keepdims=True), out)
    payload[...] = out


def sum_rows(rows):
    count = rows.shape[0]
    value = rows[pl.ds(0, 8), :]
    error = jnp.zeros_like(value)
    for at in range(8, count, 8):
        value, extra = two_sum(value, rows[pl.ds(at, 8), :])
        error = error + extra
    for step in (4, 2, 1):
        value, extra = two_sum(value, pltpu.roll(value, step, 0))
        error = error + pltpu.roll(error, step, 0) + extra
    lane = lane_of((8, LANES))
    shifted = pltpu.roll(error, LOW_LANE - MOMENT_LANE, 1)
    return value + jnp.where(lane < MOMENT_LANE, error, 0.0) + jnp.where(lane >= LOW_LANE, shifted, 0.0)


def rows_kernel(rows, out):
    out[...] = sum_rows(rows)


def fold(moments, lane):
    total = jnp.zeros_like(moments)
    for j in range(1, 2 * DEGREE + 1):
        total = jnp.where(lane == LOW_LANE - j, moments[:, j : j + 1], total)
    return jnp.where(lane >= LOW_LANE, pltpu.roll(moments, LOW_LANE, 1), total)


def shift(row, amount):
    return pltpu.roll(row, (-amount) % LANES, 1)


def apply_operator(coeffs):
    count = len(coeffs)
    terms = [[] for _ in range(count + 1)]
    for j, value in enumerate(coeffs):
        terms[j].append(dd_add(dd_scale(value, 8.0), dd_neg(value)))
        if j == 0:
            terms[1].append(dd_scale(value, 8.0))
        else:
            terms[j + 1].append(dd_scale(value, 4.0))
            terms[j - 1].append(dd_scale(value, 4.0))
    return [dd_sum(group) for group in terms]


def multiply(left, right):
    terms = [[] for _ in range(len(left) + len(right) - 1)]
    for i, a in enumerate(left):
        for j, b in enumerate(right):
            half = dd_scale(dd_mul(a, b), 0.5)
            terms[i + j].append(half)
            terms[abs(i - j)].append(half)
    return [dd_sum(group) for group in terms]


def square(values):
    terms = [[] for _ in range(2 * len(values) - 1)]
    for i, a in enumerate(values):
        for j in range(i, len(values)):
            term = dd_mul(a, values[j])
            if i == j:
                term = dd_scale(term, 0.5)
            terms[i + j].append(term)
            terms[j - i].append(term)
    return [dd_sum(group) for group in terms]


def galerkin(folded):
    high, low = folded
    moment = high + low
    beside = dd_add((shift(high, 1), shift(low, 1)), (shift(high, -1), shift(low, -1)))
    eight = dd_scale(folded, 8.0)
    weight = dd_add(dd_add(dd_scale(beside, 4.0), eight), dd_neg(folded))
    weight = weight[0] + weight[1]

    def entry(source, j):
        return jnp.broadcast_to(source[:, LOW_LANE + j : LOW_LANE + j + 1], source.shape)

    weights = [entry(weight, j) for j in range(7)]
    rhs = [entry(moment, j) for j in range(4)]
    matrix = [[0.5 * (weights[i + j] + weights[abs(i - j)]) for j in range(4)] for i in range(4)]
    for k in range(4):
        for i in range(k + 1, 4):
            factor = matrix[i][k] / matrix[k][k]
            for j in range(k + 1, i + 1):
                matrix[i][j] = matrix[i][j] - factor * matrix[j][k]
            rhs[i] = rhs[i] - factor * rhs[k]
    result = [None] * 4
    for i in range(3, -1, -1):
        value = rhs[i]
        for j in range(i + 1, 4):
            value = value - matrix[j][i] * result[j]
        result[i] = value / matrix[i][i]
    return result


def final_kernel(rows, basis, last, conductance, level, solution, residual, flow, scale=1.0):
    row = sum_rows(rows)
    lane = lane_of((8, LANES))
    high = pltpu.roll(row, LANES - MOMENT_LANE, 1)
    low = pltpu.roll(row, LANES - LOW_LANE, 1)
    valid = lane <= 2 * DEGREE
    high, low = quick_two_sum(jnp.where(valid, high, 0.0), jnp.where(valid, low, 0.0))
    first = (high[:, 0:1], low[:, 0:1])
    second = (high[:, 1:2], low[:, 1:2])
    even = lane % 2 == 0
    base = (jnp.where(even, first[0], second[0]), jnp.where(even, first[1], second[1]))
    twice = dd_add(dd_scale((high, low), 2.0), dd_neg(base))
    mu = tuple(jnp.where(valid, value, 0.0) for value in twice)
    mu = (fold(mu[0], lane), fold(mu[1], lane))
    zero = jnp.zeros((8, LANES), jnp.float32)
    first_coeffs = galerkin(mu)
    change = apply_operator([(value, zero) for value in first_coeffs])
    poly = [dd_neg(value) for value in change]
    poly[0] = dd_add(poly[0], (zero + 1.0, zero))
    nu = None
    for c, value in enumerate(square(poly)):
        if c == 0:
            overlap = mu
        else:
            up = (shift(mu[0], c), shift(mu[1], c))
            down = (shift(mu[0], -c), shift(mu[1], -c))
            overlap = dd_scale(dd_add(up, down), 0.5)
        term = dd_mul(value, overlap)
        nu = term if nu is None else dd_add(nu, term)
    second_coeffs = galerkin(nu)
    gain = multiply([(value, zero) for value in second_coeffs], poly)
    drop = apply_operator(gain)
    solved = list(gain)
    for j in range(4):
        solved[j] = dd_add(gain[j], (first_coeffs[j], zero))
    left = [dd_neg(value) for value in drop]
    for j in range(5):
        left[j] = dd_add(left[j], poly[j])
    solved = [value[0] + value[1] for value in solved]
    left = [value[0] + value[1] for value in left]

    cells = solution.shape[0]
    for at in range(0, cells, 8):
        fields = [basis[pl.ds(at * FIELDS + k, 8, stride=FIELDS), :] for k in range(FIELDS)]
        fields.append(last[pl.ds(at, 8), :])
        total = solved[0] * fields[0]
        rest = left[0] * fields[0]
        for k in range(1, DEGREE + 1):
            if k < FIELDS:
                total = total + solved[k] * fields[k]
            rest = rest + left[k] * fields[k]
        solution[pl.ds(at, 8), :] = total
        residual[pl.ds(at, 8), :] = rest

    weights = zero
    for k in range(FIELDS):
        weights = jnp.where(lane % FIELDS == k, solved[k], weights)
    header = row * weights
    for step in (4, 2, 1):
        header = header + shift(header, step)
    for q in range(OWNED):
        flow[q] = conductance[q] * (header[0, q * FIELDS] * scale - level[q])


VMEM = pl.BlockSpec(memory_space=pltpu.VMEM)
SMEM = pl.BlockSpec(memory_space=pltpu.SMEM)


def on_device(right_side, diagonal, inlet_index, plate_order, conductance, plate_level):
    cz, cy, nx = right_side.shape
    slabs, tiles = lax.axis_size("slab"), lax.axis_size("tile")
    plates, inlets = inlet_index.shape[2:]
    f32 = jnp.float32

    def both_ways(to_next, to_previous, axis):
        count = lax.axis_size(axis)
        forward = [(i, i + 1) for i in range(count - 1)]
        backward = [(target, source) for source, target in forward]
        return lax.ppermute(to_next, axis, forward), lax.ppermute(to_previous, axis, backward)

    own = jnp.stack([right_side, diagonal])
    before, after = both_ways(own[:, :, cy - HALO :], own[:, :, :HALO], "tile")
    own = jnp.concatenate([before, own, after], axis=2)
    low, high = both_ways(own, own, "slab")

    wide = (3 * cz, cy + 2 * HALO, nx)
    cells = cz * cy
    payload, basis, last = pl.pallas_call(
        basis_kernel,
        out_shape=(
            jax.ShapeDtypeStruct((tiles, LANES), f32),
            jax.ShapeDtypeStruct((cells * FIELDS, nx), f32),
            jax.ShapeDtypeStruct((cells, nx), f32),
        ),
        in_specs=[VMEM, VMEM, VMEM, SMEM, SMEM],
        out_specs=(VMEM, VMEM, VMEM),
        scratch_shapes=[
            pltpu.VMEM(wide, f32),
            pltpu.VMEM(wide, f32),
            pltpu.VMEM(wide, f32),
            pltpu.VMEM(wide, f32),
            pltpu.VMEM((24 * 8, nx), f32),
            pltpu.VMEM((plates * FIELDS, nx), f32),
        ],
        compiler_params=pltpu.CompilerParams(vmem_limit_bytes=32 * 1024 * 1024),
        name="basis",
    )(own, low, high, inlet_index.reshape(plates * inlets), plate_order)

    arrived = lax.all_to_all(payload.reshape(tiles, 1, LANES), "tile", 0, 0, tiled=True)
    row = pl.pallas_call(
        rows_kernel,
        out_shape=jax.ShapeDtypeStruct((8, LANES), f32),
        in_specs=[VMEM],
        out_specs=VMEM,
        name="rows",
    )(arrived.reshape(tiles, LANES))
    copies = jnp.broadcast_to(row[:1, None, :], (slabs, 1, LANES))
    arrived = lax.all_to_all(copies, "slab", 0, 0, tiled=True)
    arrived = arrived.reshape(slabs, LANES)
    if slabs % 8:
        arrived = jnp.pad(arrived, ((0, 8 - slabs % 8), (0, 0)))
    scale = float(1.0 / (slabs * tiles * inlets) ** 0.5)
    solution, residual, flow = pl.pallas_call(
        functools.partial(final_kernel, scale=scale),
        out_shape=(
            jax.ShapeDtypeStruct((cells, nx), f32),
            jax.ShapeDtypeStruct((cells, nx), f32),
            jax.ShapeDtypeStruct((OWNED,), f32),
        ),
        in_specs=[VMEM, VMEM, VMEM, SMEM, SMEM],
        out_specs=(VMEM, VMEM, SMEM),
        compiler_params=pltpu.CompilerParams(vmem_limit_bytes=16 * 1024 * 1024),
        name="final",
    )(arrived, basis, last, conductance, plate_level)
    return (solution.reshape(cz, cy, nx), residual.reshape(cz, cy, nx), flow)


def solution(mesh):
    in_specs = (
        P("slab", "tile", None),
        P("slab", "tile", None),
        P("slab", "tile", None, None),
        P(),
        P("tile"),
        P("tile"),
    )
    out_specs = (P("slab", "tile", None), P("slab", "tile", None), P("tile"))
    return jax.shard_map(
        on_device, mesh=mesh, in_specs=in_specs, out_specs=out_specs, check_vma=False
    )
```

```python
import functools

import jax
import jax.numpy as jnp
from jax import lax
from jax.experimental import pallas as pl
from jax.experimental.pallas import tpu as pltpu
from jax.sharding import PartitionSpec as P

HALO = 8
DEGREE = 8
FIELDS = 8
OWNED = 4
LANES = 128
MOMENT_LANE = 32
LOW_LANE = 64
SLAB = ("x", "core")
TILE = ("z", "y")


def two_sum(a, b):
    s = a + b
    v = s - a
    return s, (a - (s - v)) + (b - v)


def quick_two_sum(a, b):
    s = a + b
    return s, b - (s - a)


def split(a):
    c = a * 4097.0
    high = c - (c - a)
    return high, a - high


def two_prod(a, b):
    p = a * b
    ah, al = split(a)
    bh, bl = split(b)
    return p, ((ah * bh - p) + ah * bl + al * bh) + al * bl


def dd_add(x, y):
    s, e = two_sum(x[0], y[0])
    t, f = two_sum(x[1], y[1])
    s, e = quick_two_sum(s, e + t)
    return quick_two_sum(s, e + f)


def dd_mul(x, y):
    p, e = two_prod(x[0], y[0])
    return quick_two_sum(p, e + (x[0] * y[1] + x[1] * y[0]))


def dd_scale(x, power):
    return x[0] * power, x[1] * power


def dd_neg(x):
    return -x[0], -x[1]


def dd_sum(terms):
    total = terms[0]
    for term in terms[1:]:
        total = dd_add(total, term)
    return total


def lane_of(shape):
    return lax.broadcasted_iota(jnp.int32, shape, len(shape) - 1)


def prepare_kernel(index, order, conductance, level, hot, table, plate_of, owner):
    plate_of[...] = order[...]
    cells = index[...]
    inlets, plates = cells.shape
    lane = lane_of((inlets, LANES))
    slot = lax.broadcasted_iota(jnp.int32, (inlets, LANES), 0)
    packed = LANES // inlets
    for row in range(plates // packed):
        total = jnp.zeros((inlets, LANES), jnp.int32)
        for place in range(packed):
            at = row * packed + place
            cell = jnp.broadcast_to(cells[:, at : at + 1], (inlets, LANES))
            hot[pl.ds(at * inlets, inlets), :] = jnp.where(lane == (cell & 127), 1.0, 0.0)
            total = total + jnp.where(lane == slot + place * inlets, (cell >> 7) * FIELDS, 0)
        table[pl.ds(row, 1), :] = jnp.sum(total, axis=0, keepdims=True)
    lane = lane_of((8, LANES))
    first = lax.broadcasted_iota(jnp.int32, (8, LANES), 0) == 0
    values = jnp.zeros((8, LANES), jnp.float32)
    for q in range(OWNED):
        values = jnp.where(lane == q * FIELDS, jnp.where(first, conductance[q], level[q]), values)
    owner[...] = values


def basis_kernel(
    own, low, high, hot, table, order, payload, basis, last,
    alpha, beta, even, odd, parts, sums, index, plate_of, arrivals,
):
    copies = [
        pltpu.make_async_copy(table, index, arrivals.at[0]),
        pltpu.make_async_copy(order, plate_of, arrivals.at[1]),
    ]
    for copy in copies:
        copy.start()
    cz = own.shape[1]
    wide_y = own.shape[2]
    cy = wide_y - 2 * HALO
    for place, source in enumerate((low, own, high)):
        at = pl.ds(place * cz, cz)
        even[at, HALO : HALO + wide_y, :] = source[0]
        diag = source[1]
        inside = jnp.where(diag > 0.0, 0.25, 0.0)
        beta[at] = inside
        alpha[at] = (diag - 1.0) * inside
    lane = lane_of((wide_y, LANES))
    planes = 3 * cz
    edge = jnp.zeros((planes, HALO, LANES), jnp.float32)
    for field in (even, odd):
        field[:, :HALO, :] = edge
        field[:, HALO + wide_y :, :] = edge
    rows = pl.ds(HALO, wide_y)
    inner = pl.ds(2 * HALO, cy)

    def emit(field, degree):
        for z in range(cz):
            value = field[cz + z, inner, :]
            if degree < FIELDS:
                basis[pl.ds(z * cy * FIELDS + degree, cy, stride=FIELDS), :] = value
            else:
                last[pl.ds(z * cy, cy), :] = value

    def product(first, second, slot):
        total = None
        for z in range(cz):
            term = first[cz + z, inner, :] * second[cz + z, inner, :]
            term = term[:8] + term[8:]
            total = term if total is None else total + term
        parts[pl.ds(slot * 8, 8), :] = total

    emit(even, 0)
    product(even, even, 0)
    now, later = even, odd
    for degree in range(DEGREE):

        def plane(z, now=now, later=later, degree=degree):
            value = now[z, rows, :]
            beside = now[z - 1, rows, :] + now[z + 1, rows, :]
            beside = beside + now[z, pl.ds(HALO - 1, wide_y), :] + now[z, pl.ds(HALO + 1, wide_y), :]
            beside = beside + jnp.where(lane == 0, 0.0, pltpu.roll(value, 1, 1))
            beside = beside + jnp.where(lane == LANES - 1, 0.0, pltpu.roll(value, LANES - 1, 1))
            fresh = alpha[z] * value - beta[z] * beside
            if degree == 0:
                later[z, rows, :] = 0.5 * fresh
            else:
                later[z, rows, :] = fresh - later[z, rows, :]

        for z in range(degree + 1, planes - 1 - degree):
            plane(z)
        emit(later, degree + 1)
        product(now, later, 2 * degree + 1)
        product(later, later, 2 * degree + 2)
        now, later = later, now

    slots = parts.shape[0] // 8
    for slot in range(2 * DEGREE + 1, slots):
        parts[pl.ds(slot * 8, 8), :] = jnp.zeros((8, LANES), jnp.float32)
    value = parts[pl.ds(0, slots, stride=8), :]
    error = jnp.zeros_like(value)
    for row in range(1, 8):
        value, extra = two_sum(value, parts[pl.ds(row, slots, stride=8), :])
        error = error + extra
    step = LANES // 2
    while step:
        value, extra = two_sum(value, pltpu.roll(value, step, 1))
        error = error + pltpu.roll(error, step, 1) + extra
        step //= 2
    value, error = quick_two_sum(value, error)
    lane_s = lane_of((slots, LANES))
    row_s = lax.broadcasted_iota(jnp.int32, (slots, LANES), 0)
    placed = jnp.where(lane_s == MOMENT_LANE + row_s, value, 0.0)
    placed = placed + jnp.where(lane_s == LOW_LANE + row_s, error, 0.0)
    moments = jnp.sum(placed, axis=0, keepdims=True)

    for copy in copies:
        copy.wait()
    plates = sums.shape[0] // FIELDS
    inlets = hot.shape[0] // plates

    def plate(at, carry):
        of = plate_of[at]
        start = pl.multiple_of(of * inlets, inlets)
        line, place = of >> 3, (of & 7) * inlets
        totals = [None, None]
        for slot in range(inlets):
            row = pl.multiple_of(index[line, place + slot], FIELDS)
            picked = basis[pl.ds(row, FIELDS), :] * hot[pl.ds(start + slot, FIELDS, stride=0), :]
            side = slot % 2
            totals[side] = picked if totals[side] is None else totals[side] + picked
        sums[pl.ds(pl.multiple_of(at * FIELDS, FIELDS), FIELDS), :] = totals[0] + totals[1]
        return carry

    lax.fori_loop(0, plates, plate, 0, unroll=8)
    tiles = plates // OWNED
    lane_t = lane_of((tiles, LANES))
    out = jnp.broadcast_to(moments, (tiles, LANES))
    for slot in range(OWNED * FIELDS):
        column = sums[pl.ds(slot, tiles, stride=OWNED * FIELDS), :]
        out = jnp.where(lane_t == slot, jnp.sum(column, axis=1, keepdims=True), out)
    for at in range(0, payload.shape[0], tiles):
        payload[pl.ds(at, tiles), :] = out


def with_error(value, error):
    lane = lane_of(value.shape)
    shifted = pltpu.roll(error, LOW_LANE - MOMENT_LANE, 1)
    return value + jnp.where(lane < MOMENT_LANE, error, 0.0) + jnp.where(lane >= LOW_LANE, shifted, 0.0)


def sum_rows(rows):
    count = rows.shape[0]
    value = rows[pl.ds(0, 8), :]
    error = jnp.zeros_like(value)
    for at in range(8, count, 8):
        value, extra = two_sum(value, rows[pl.ds(at, 8), :])
        error = error + extra
    for step in (4, 2, 1):
        value, extra = two_sum(value, pltpu.roll(value, step, 0))
        error = error + pltpu.roll(error, step, 0) + extra
    return with_error(value, error)


def rows_kernel(rows, out):
    count = out.shape[0] // 2
    value = rows[pl.ds(0, count), :]
    error = jnp.zeros_like(value)
    for at in range(count, rows.shape[0], count):
        value, extra = two_sum(value, rows[pl.ds(at, count), :])
        error = error + extra
    value = with_error(value, error)
    out[pl.ds(0, count), :] = value
    out[pl.ds(count, count), :] = value


def fold(moments, lane):
    total = jnp.zeros_like(moments)
    for j in range(1, 2 * DEGREE + 1):
        total = jnp.where(lane == LOW_LANE - j, moments[:, j : j + 1], total)
    return jnp.where(lane >= LOW_LANE, pltpu.roll(moments, LOW_LANE, 1), total)


def shift(row, amount):
    return pltpu.roll(row, (-amount) % LANES, 1)


def apply_operator(coeffs):
    count = len(coeffs)
    terms = [[] for _ in range(count + 1)]
    for j, value in enumerate(coeffs):
        terms[j].append(dd_add(dd_scale(value, 8.0), dd_neg(value)))
        if j == 0:
            terms[1].append(dd_scale(value, 8.0))
        else:
            terms[j + 1].append(dd_scale(value, 4.0))
            terms[j - 1].append(dd_scale(value, 4.0))
    return [dd_sum(group) for group in terms]


def multiply(left, right):
    terms = [[] for _ in range(len(left) + len(right) - 1)]
    for i, a in enumerate(left):
        for j, b in enumerate(right):
            half = dd_scale(dd_mul(a, b), 0.5)
            terms[i + j].append(half)
            terms[abs(i - j)].append(half)
    return [dd_sum(group) for group in terms]


def square(values):
    terms = [[] for _ in range(2 * len(values) - 1)]
    for i, a in enumerate(values):
        for j in range(i, len(values)):
            term = dd_mul(a, values[j])
            if i == j:
                term = dd_scale(term, 0.5)
            terms[i + j].append(term)
            terms[j - i].append(term)
    return [dd_sum(group) for group in terms]


def galerkin(folded):
    high, low = folded
    moment = high + low
    beside = dd_add((shift(high, 1), shift(low, 1)), (shift(high, -1), shift(low, -1)))
    eight = dd_scale(folded, 8.0)
    weight = dd_add(dd_add(dd_scale(beside, 4.0), eight), dd_neg(folded))
    weight = weight[0] + weight[1]

    def entry(source, j):
        return jnp.broadcast_to(source[:, LOW_LANE + j : LOW_LANE + j + 1], source.shape)

    weights = [entry(weight, j) for j in range(7)]
    rhs = [entry(moment, j) for j in range(4)]
    matrix = [[0.5 * (weights[i + j] + weights[abs(i - j)]) for j in range(4)] for i in range(4)]
    for k in range(4):
        for i in range(k + 1, 4):
            factor = matrix[i][k] / matrix[k][k]
            for j in range(k + 1, i + 1):
                matrix[i][j] = matrix[i][j] - factor * matrix[j][k]
            rhs[i] = rhs[i] - factor * rhs[k]
    result = [None] * 4
    for i in range(3, -1, -1):
        value = rhs[i]
        for j in range(i + 1, 4):
            value = value - matrix[j][i] * result[j]
        result[i] = value / matrix[i][i]
    return result


def final_kernel(rows, basis, last, owner, solution, residual, flow, scale=1.0):
    row = sum_rows(rows)
    lane = lane_of((8, LANES))
    high = pltpu.roll(row, LANES - MOMENT_LANE, 1)
    low = pltpu.roll(row, LANES - LOW_LANE, 1)
    valid = lane <= 2 * DEGREE
    high, low = quick_two_sum(jnp.where(valid, high, 0.0), jnp.where(valid, low, 0.0))
    first = (high[:, 0:1], low[:, 0:1])
    second = (high[:, 1:2], low[:, 1:2])
    even = lane % 2 == 0
    base = (jnp.where(even, first[0], second[0]), jnp.where(even, first[1], second[1]))
    twice = dd_add(dd_scale((high, low), 2.0), dd_neg(base))
    mu = tuple(jnp.where(valid, value, 0.0) for value in twice)
    mu = (fold(mu[0], lane), fold(mu[1], lane))
    zero = jnp.zeros((8, LANES), jnp.float32)
    first_coeffs = galerkin(mu)
    change = apply_operator([(value, zero) for value in first_coeffs])
    poly = [dd_neg(value) for value in change]
    poly[0] = dd_add(poly[0], (zero + 1.0, zero))
    nu = None
    for c, value in enumerate(square(poly)):
        if c == 0:
            overlap = mu
        else:
            up = (shift(mu[0], c), shift(mu[1], c))
            down = (shift(mu[0], -c), shift(mu[1], -c))
            overlap = dd_scale(dd_add(up, down), 0.5)
        term = dd_mul(value, overlap)
        nu = term if nu is None else dd_add(nu, term)
    second_coeffs = galerkin(nu)
    gain = multiply([(value, zero) for value in second_coeffs], poly)
    drop = apply_operator(gain)
    solved = list(gain)
    for j in range(4):
        solved[j] = dd_add(gain[j], (first_coeffs[j], zero))
    left = [dd_neg(value) for value in drop]
    for j in range(5):
        left[j] = dd_add(left[j], poly[j])
    solved = [value[0] + value[1] for value in solved]
    left = [value[0] + value[1] for value in left]

    cells = solution.shape[0]
    for at in range(0, cells, 8):
        fields = [basis[pl.ds(at * FIELDS + k, 8, stride=FIELDS), :] for k in range(FIELDS)]
        fields.append(last[pl.ds(at, 8), :])
        total = solved[0] * fields[0]
        rest = left[0] * fields[0]
        for k in range(1, DEGREE + 1):
            if k < FIELDS:
                total = total + solved[k] * fields[k]
            rest = rest + left[k] * fields[k]
        solution[pl.ds(at, 8), :] = total
        residual[pl.ds(at, 8), :] = rest

    weights = zero
    for k in range(FIELDS):
        weights = jnp.where(lane % FIELDS == k, solved[k], weights)
    header = row * weights
    for step in (4, 2, 1):
        header = header + shift(header, step)
    result = owner[0:1, :] * (header[0:1, :] * scale - owner[1:2, :])
    for q in range(OWNED):
        flow[q] = result[0, q * FIELDS]


VMEM = pl.BlockSpec(memory_space=pltpu.VMEM)
SMEM = pl.BlockSpec(memory_space=pltpu.SMEM)


def on_device(right_side, diagonal, inlet_index, plate_order, conductance, plate_level):
    cz, cy, nx = right_side.shape
    tiles = lax.axis_size(TILE)
    devices = lax.axis_size(SLAB) * tiles
    plates, inlets = inlet_index.shape[2:]
    f32 = jnp.float32

    def both_ways(to_next, to_previous, axis):
        count = lax.axis_size(axis)
        forward = [(i, i + 1) for i in range(count - 1)]
        backward = [(target, source) for source, target in forward]
        return lax.ppermute(to_next, axis, forward), lax.ppermute(to_previous, axis, backward)

    own = jnp.stack([right_side, diagonal])
    before, after = both_ways(own[:, :, cy - HALO :], own[:, :, :HALO], TILE)
    own = jnp.concatenate([before, own, after], axis=2)
    low, high = both_ways(own, own, SLAB)

    hot, table, order, owner = pl.pallas_call(
        prepare_kernel,
        out_shape=(
            jax.ShapeDtypeStruct((plates * inlets, LANES), f32),
            jax.ShapeDtypeStruct((plates * inlets // LANES, LANES), jnp.int32),
            jax.ShapeDtypeStruct((plates,), jnp.int32),
            jax.ShapeDtypeStruct((8, LANES), f32),
        ),
        in_specs=[VMEM, VMEM, SMEM, SMEM],
        out_specs=(VMEM,) * 4,
        compiler_params=pltpu.CompilerParams(vmem_limit_bytes=4 * 1024 * 1024),
        cost_estimate=pl.CostEstimate(flops=800000, bytes_accessed=3200000, transcendentals=0),
        name="prepare",
    )(inlet_index[0, 0].T, plate_order, conductance, plate_level)

    wide = (3 * cz, cy + 2 * HALO, nx)
    tall = (wide[0], wide[1] + 2 * HALO, nx)
    cells = cz * cy
    copies = lax.axis_size("x")
    payload, basis, last = pl.pallas_call(
        basis_kernel,
        out_shape=(
            jax.ShapeDtypeStruct((copies * tiles, LANES), f32),
            jax.ShapeDtypeStruct((cells * FIELDS, nx), f32),
            jax.ShapeDtypeStruct((cells, nx), f32),
        ),
        in_specs=[VMEM] * 6,
        out_specs=(VMEM, VMEM, VMEM),
        scratch_shapes=[
            pltpu.VMEM(wide, f32),
            pltpu.VMEM(wide, f32),
            pltpu.VMEM(tall, f32),
            pltpu.VMEM(tall, f32),
            pltpu.VMEM((24 * 8, nx), f32),
            pltpu.VMEM((plates * FIELDS, nx), f32),
            pltpu.SMEM((plates * inlets // LANES, LANES), jnp.int32),
            pltpu.SMEM((plates,), jnp.int32),
            pltpu.SemaphoreType.DMA((2,)),
        ],
        compiler_params=pltpu.CompilerParams(vmem_limit_bytes=8 * 1024 * 1024),
        name="basis",
    )(own, low, high, hot, table, order)

    group = copies * lax.axis_size("z")
    width = lax.axis_size("y")
    arrived = lax.all_to_all(payload.reshape(group, width, LANES), ("x", "z"), 0, 0, tiled=True)
    ends = lax.axis_size("core") * width
    rows = pl.pallas_call(
        rows_kernel,
        out_shape=jax.ShapeDtypeStruct((ends, LANES), f32),
        in_specs=[VMEM],
        out_specs=VMEM,
        compiler_params=pltpu.CompilerParams(vmem_limit_bytes=2 * 1024 * 1024),
        name="rows",
    )(arrived.reshape(group * width, LANES))
    arrived = lax.all_to_all(rows.reshape(ends, 1, LANES), ("core", "y"), 0, 0, tiled=True)
    scale = float(1.0 / (devices * inlets) ** 0.5)
    solution, residual, flow = pl.pallas_call(
        functools.partial(final_kernel, scale=scale),
        out_shape=(
            jax.ShapeDtypeStruct((cells, nx), f32),
            jax.ShapeDtypeStruct((cells, nx), f32),
            jax.ShapeDtypeStruct((OWNED,), f32),
        ),
        in_specs=[VMEM, VMEM, VMEM, VMEM],
        out_specs=(VMEM, VMEM, SMEM),
        compiler_params=pltpu.CompilerParams(vmem_limit_bytes=4 * 1024 * 1024),
        name="final",
    )(arrived.reshape(ends, LANES), basis, last, owner)
    return (solution.reshape(cz, cy, nx), residual.reshape(cz, cy, nx), flow)


def solution(mesh):
    slabs, tiles = mesh.devices.shape
    chips = mesh.devices.reshape(slabs // 2, 2, tiles // 8, 8)
    fine = jax.sharding.Mesh(chips, SLAB + TILE)
    in_specs = (
        P(SLAB, TILE, None),
        P(SLAB, TILE, None),
        P(SLAB, TILE, None, None),
        P(),
        P(TILE),
        P(TILE),
    )
    out_specs = (P(SLAB, TILE, None), P(SLAB, TILE, None), P(TILE))
    return jax.shard_map(
        on_device, mesh=fine, in_specs=in_specs, out_specs=out_specs, check_vma=False
    )
```

```python
import functools

import jax
import jax.numpy as jnp
from jax import lax
from jax.experimental import pallas as pl
from jax.experimental.pallas import tpu as pltpu
from jax.sharding import PartitionSpec as P

HALO = 8
DEGREE = 8
FIELDS = 8
OWNED = 4
WIDTH = 8
PACKED = 4
LANES = 128
HIGH_LANE = 48
LOW_LANE = 96
CENTER = 64
SLAB = ("x", "core")
TILE = ("z", "y")


def two_sum(a, b):
    s = a + b
    v = s - a
    return s, (a - (s - v)) + (b - v)


def quick_two_sum(a, b):
    s = a + b
    return s, b - (s - a)


def split(a):
    c = a * 4097.0
    high = c - (c - a)
    return high, a - high


def two_prod(a, b):
    p = a * b
    ah, al = split(a)
    bh, bl = split(b)
    return p, ((ah * bh - p) + ah * bl + al * bh) + al * bl


def dd_add(x, y):
    s, e = two_sum(x[0], y[0])
    t, f = two_sum(x[1], y[1])
    s, e = quick_two_sum(s, e + t)
    return quick_two_sum(s, e + f)


def dd_mul(x, y):
    p, e = two_prod(x[0], y[0])
    return quick_two_sum(p, e + (x[0] * y[1] + x[1] * y[0]))


def dd_scale(x, power):
    return x[0] * power, x[1] * power


def dd_neg(x):
    return -x[0], -x[1]


def dd_sum(terms):
    total = terms[0]
    for term in terms[1:]:
        total = dd_add(total, term)
    return total


def lane_of(shape):
    return lax.broadcasted_iota(jnp.int32, shape, len(shape) - 1)


def prepare_kernel(index, order, conductance, level, hot, table, plate_of, owner, cells, factor, offset, arrivals):
    copies = [
        pltpu.make_async_copy(source, target, arrivals.at[at])
        for at, (source, target) in enumerate(
            ((index, cells), (order, plate_of), (conductance, factor), (level, offset))
        )
    ]
    for copy in copies:
        copy.start()
    for copy in copies:
        copy.wait()
    cells = cells[...]
    inlets, plates = cells.shape
    lane = lane_of((inlets, LANES))
    slot = lax.broadcasted_iota(jnp.int32, (inlets, LANES), 0)
    packed = LANES // inlets
    for row in range(plates // packed):
        total = jnp.zeros((inlets, LANES), jnp.int32)
        for place in range(packed):
            at = row * packed + place
            cell = jnp.broadcast_to(cells[:, at : at + 1], (inlets, LANES))
            hot[pl.ds(at * inlets, inlets), :] = jnp.where(lane == (cell & 127), 1.0, 0.0)
            total = total + jnp.where(lane == slot + place * inlets, (cell >> 7) * FIELDS, 0)
        table[pl.ds(row, 1), :] = jnp.sum(total, axis=0, keepdims=True)
    lane = lane_of((8, LANES))
    first = lax.broadcasted_iota(jnp.int32, (8, LANES), 0) == 0
    values = jnp.zeros((8, LANES), jnp.float32)
    for q in range(OWNED):
        values = jnp.where(lane == q * FIELDS, jnp.where(first, factor[q], offset[q]), values)
    owner[...] = values


def basis_kernel(
    own, low, high, hot, table, order, payload, basis, last,
    alpha, beta, even, odd, parts, sums, index, plate_of, arrivals,
):
    copies = [
        pltpu.make_async_copy(table, index, arrivals.at[0]),
        pltpu.make_async_copy(order, plate_of, arrivals.at[1]),
    ]
    for copy in copies:
        copy.start()
    cz = own.shape[1]
    wide_y = own.shape[2]
    cy = wide_y - 2 * HALO
    for place, source in enumerate((low, own, high)):
        at = pl.ds(place * cz, cz)
        even[at, HALO : HALO + wide_y, :] = source[0]
        diag = source[1]
        inside = jnp.where(diag > 0.0, 0.25, 0.0)
        beta[at] = inside
        alpha[at] = (diag - 1.0) * inside
    lane = lane_of((wide_y, LANES))
    planes = 3 * cz
    edge = jnp.zeros((planes, HALO, LANES), jnp.float32)
    for field in (even, odd):
        field[:, :HALO, :] = edge
        field[:, HALO + wide_y :, :] = edge
    rows = pl.ds(HALO, wide_y)
    inner = pl.ds(2 * HALO, cy)

    def emit(field, degree):
        for z in range(cz):
            value = field[cz + z, inner, :]
            if degree < FIELDS:
                basis[pl.ds(z * cy * FIELDS + degree, cy, stride=FIELDS), :] = value
            else:
                last[pl.ds(z * cy, cy), :] = value

    def product(first, second, slot):
        total = None
        for z in range(cz):
            term = first[cz + z, inner, :] * second[cz + z, inner, :]
            term = term[:8] + term[8:]
            total = term if total is None else total + term
        parts[pl.ds(slot * 8, 8), :] = total

    emit(even, 0)
    product(even, even, 0)
    now, later = even, odd
    for degree in range(DEGREE):

        def plane(z, now=now, later=later, degree=degree):
            value = now[z, rows, :]
            beside = now[z - 1, rows, :] + now[z + 1, rows, :]
            beside = beside + now[z, pl.ds(HALO - 1, wide_y), :] + now[z, pl.ds(HALO + 1, wide_y), :]
            beside = beside + jnp.where(lane == 0, 0.0, pltpu.roll(value, 1, 1))
            beside = beside + jnp.where(lane == LANES - 1, 0.0, pltpu.roll(value, LANES - 1, 1))
            fresh = alpha[z] * value - beta[z] * beside
            if degree == 0:
                later[z, rows, :] = 0.5 * fresh
            else:
                later[z, rows, :] = fresh - later[z, rows, :]

        for z in range(degree + 1, planes - 1 - degree):
            plane(z)
        emit(later, degree + 1)
        product(now, later, 2 * degree + 1)
        product(later, later, 2 * degree + 2)
        now, later = later, now

    slots = parts.shape[0] // 8
    for slot in range(2 * DEGREE + 1, slots):
        parts[pl.ds(slot * 8, 8), :] = jnp.zeros((8, LANES), jnp.float32)
    value = parts[pl.ds(0, slots, stride=8), :]
    error = jnp.zeros_like(value)
    for row in range(1, 8):
        value, extra = two_sum(value, parts[pl.ds(row, slots, stride=8), :])
        error = error + extra
    step = LANES // 2
    while step:
        value, extra = two_sum(value, pltpu.roll(value, step, 1))
        error = error + pltpu.roll(error, step, 1) + extra
        step //= 2
    lane_s = lane_of((slots, LANES))
    row_s = lax.broadcasted_iota(jnp.int32, (slots, LANES), 0)
    parity = row_s % 2 == 0
    base = jnp.where(parity, value[0:1], value[1:2])
    base_error = jnp.where(parity, error[0:1], error[1:2])
    value, extra = two_sum(2.0 * value, -base)
    error = (2.0 * error - base_error) + extra
    value, error = quick_two_sum(value, error)
    placed = jnp.where(jnp.abs(lane_s - HIGH_LANE) == row_s, value, 0.0)
    placed = placed + jnp.where(jnp.abs(lane_s - LOW_LANE) == row_s, error, 0.0)
    placed = jnp.where(row_s <= 2 * DEGREE, placed, 0.0)
    moments = jnp.sum(placed, axis=0, keepdims=True)

    for copy in copies:
        copy.wait()
    plates = sums.shape[0] // FIELDS
    inlets = index.shape[0] // plates

    def plate(at, carry):
        start = pl.multiple_of(plate_of[at] * inlets, inlets)
        totals = [None, None]
        for slot in range(inlets):
            row = pl.multiple_of(index[start + slot], FIELDS)
            picked = basis[pl.ds(row, FIELDS), :] * hot[pl.ds(start + slot, FIELDS, stride=0), :]
            side = slot % 2
            totals[side] = picked if totals[side] is None else totals[side] + picked
        sums[pl.ds(pl.multiple_of(at * FIELDS, FIELDS), FIELDS), :] = totals[0] + totals[1]
        return carry

    lax.fori_loop(0, plates, plate, 0, unroll=8)
    lines = plates // (OWNED * WIDTH * PACKED)
    lane_w = lane_of((WIDTH, LANES))
    span = OWNED * FIELDS
    rows_per = WIDTH * (lines + 1)
    sources = payload.shape[0] // rows_per

    for line in range(lines):
        out = jnp.zeros((WIDTH, LANES), jnp.float32)
        for at in range(LANES):
            place, slot = divmod(at, span)
            first = (line * PACKED + place) * WIDTH * span + slot
            column = sums[pl.ds(first, WIDTH, stride=span), :]
            out = jnp.where(lane_w == at, jnp.sum(column, axis=1, keepdims=True), out)
        for at in range(sources):
            payload[pl.ds(at * rows_per + line, WIDTH, stride=lines + 1), :] = out
    out = jnp.broadcast_to(moments, (WIDTH, LANES))
    for at in range(sources):
        payload[pl.ds(at * rows_per + lines, WIDTH, stride=lines + 1), :] = out


def with_error(value, error):
    lane = lane_of(value.shape)
    shifted = pltpu.roll(error, LOW_LANE - HIGH_LANE, 1)
    first = lane < OWNED * FIELDS
    return value + jnp.where(first, error, 0.0) + jnp.where(lane >= LOW_LANE - 2 * DEGREE, shifted, 0.0)


def sum_rows(rows, step):
    value = rows[pl.ds(0, 8), :]
    error = jnp.zeros_like(value)
    for at in range(8, rows.shape[0], 8):
        value, extra = two_sum(value, rows[pl.ds(at, 8), :])
        error = error + extra
    while step < 8:
        value, extra = two_sum(value, pltpu.roll(value, step, 0))
        error = error + pltpu.roll(error, step, 0) + extra
        step *= 2
    return value, error


def rows_kernel(rows, out, lines=1):
    value, error = sum_rows(rows, lines + 1)
    moments = with_error(value, error)[lines : lines + 1]
    total = value + error
    depth = lines * PACKED
    row = lax.broadcasted_iota(jnp.int32, (8, LANES), 0)
    first = lane_of((1, LANES)) < OWNED * FIELDS
    made = []
    for z in range(depth):
        line = total[z // PACKED : z // PACKED + 1]
        place = (z % PACKED) * OWNED * FIELDS
        if place:
            line = pltpu.roll(line, LANES - place, 1)
        made.append(jnp.where(first, line, moments))
    for at in range(0, out.shape[0], depth):
        for z in range(depth):
            out[pl.ds(at + z, 1), :] = made[z]


def shift(row, amount):
    return pltpu.roll(row, (-amount) % LANES, 1)


def apply_operator(coeffs):
    count = len(coeffs)
    terms = [[] for _ in range(count + 1)]
    for j, value in enumerate(coeffs):
        terms[j].append(dd_add(dd_scale(value, 8.0), dd_neg(value)))
        if j == 0:
            terms[1].append(dd_scale(value, 8.0))
        else:
            terms[j + 1].append(dd_scale(value, 4.0))
            terms[j - 1].append(dd_scale(value, 4.0))
    return [dd_sum(group) for group in terms]


def multiply(left, right):
    terms = [[] for _ in range(len(left) + len(right) - 1)]
    for i, a in enumerate(left):
        for j, b in enumerate(right):
            half = dd_scale(dd_mul(a, b), 0.5)
            terms[i + j].append(half)
            terms[abs(i - j)].append(half)
    return [dd_sum(group) for group in terms]


def square(values):
    terms = [[] for _ in range(2 * len(values) - 1)]
    for i, a in enumerate(values):
        for j in range(i, len(values)):
            term = dd_mul(a, values[j])
            if i == j:
                term = dd_scale(term, 0.5)
            terms[i + j].append(term)
            terms[j - i].append(term)
    return [dd_sum(group) for group in terms]


def galerkin(folded):
    high, low = folded
    moment = high + low
    beside = dd_add((shift(high, 1), shift(low, 1)), (shift(high, -1), shift(low, -1)))
    eight = dd_scale(folded, 8.0)
    weight = dd_add(dd_add(dd_scale(beside, 4.0), eight), dd_neg(folded))
    weight = weight[0] + weight[1]

    def entry(source, j):
        return jnp.broadcast_to(source[:, CENTER + j : CENTER + j + 1], source.shape)

    weights = [entry(weight, j) for j in range(7)]
    rhs = [entry(moment, j) for j in range(4)]
    matrix = [[0.5 * (weights[i + j] + weights[abs(i - j)]) for j in range(4)] for i in range(4)]
    inverse = []
    for k in range(4):
        inverse.append(1.0 / matrix[k][k])
        for i in range(k + 1, 4):
            factor = matrix[i][k] * inverse[k]
            for j in range(k + 1, i + 1):
                matrix[i][j] = matrix[i][j] - factor * matrix[j][k]
            rhs[i] = rhs[i] - factor * rhs[k]
    result = [None] * 4
    for i in range(3, -1, -1):
        value = rhs[i]
        for j in range(i + 1, 4):
            value = value - matrix[j][i] * result[j]
        result[i] = value * inverse[i]
    return result


def final_kernel(rows, basis, last, owner, solution, residual, flow, scale=1.0):
    row = with_error(*sum_rows(rows, 1))
    lane = lane_of((8, LANES))
    valid = jnp.abs(lane - CENTER) <= 2 * DEGREE
    high = jnp.where(valid, pltpu.roll(row, CENTER - HIGH_LANE, 1), 0.0)
    low = jnp.where(valid, pltpu.roll(row, LANES + CENTER - LOW_LANE, 1), 0.0)
    mu = quick_two_sum(high, low)
    zero = jnp.zeros((8, LANES), jnp.float32)
    first_coeffs = galerkin(mu)
    change = apply_operator([(value, zero) for value in first_coeffs])
    poly = [dd_neg(value) for value in change]
    poly[0] = dd_add(poly[0], (zero + 1.0, zero))
    nu = None
    for c, value in enumerate(square(poly)):
        if c == 0:
            overlap = mu
        else:
            up = (shift(mu[0], c), shift(mu[1], c))
            down = (shift(mu[0], -c), shift(mu[1], -c))
            overlap = dd_scale(dd_add(up, down), 0.5)
        term = dd_mul(value, overlap)
        nu = term if nu is None else dd_add(nu, term)
    second_coeffs = galerkin(nu)
    gain = multiply([(value, zero) for value in second_coeffs], poly)
    drop = apply_operator(gain)
    solved = list(gain)
    for j in range(4):
        solved[j] = dd_add(gain[j], (first_coeffs[j], zero))
    left = [dd_neg(value) for value in drop]
    for j in range(5):
        left[j] = dd_add(left[j], poly[j])
    solved = [value[0] + value[1] for value in solved]
    left = [value[0] + value[1] for value in left]

    cells = solution.shape[0]
    for at in range(0, cells, 8):
        fields = [basis[pl.ds(at * FIELDS + k, 8, stride=FIELDS), :] for k in range(FIELDS)]
        fields.append(last[pl.ds(at, 8), :])
        total = solved[0] * fields[0]
        rest = left[0] * fields[0]
        for k in range(1, DEGREE + 1):
            if k < FIELDS:
                total = total + solved[k] * fields[k]
            rest = rest + left[k] * fields[k]
        solution[pl.ds(at, 8), :] = total
        residual[pl.ds(at, 8), :] = rest

    weights = zero
    for k in range(FIELDS):
        weights = jnp.where(lane % FIELDS == k, solved[k], weights)
    header = row * weights
    for step in (4, 2, 1):
        header = header + shift(header, step)
    result = owner[0:1, :] * (header[0:1, :] * scale - owner[1:2, :])
    for q in range(OWNED):
        flow[q] = result[0, q * FIELDS]


VMEM = pl.BlockSpec(memory_space=pltpu.VMEM)
SMEM = pl.BlockSpec(memory_space=pltpu.SMEM)


def on_device(right_side, diagonal, inlet_index, plate_order, conductance, plate_level):
    cz, cy, nx = right_side.shape
    tiles = lax.axis_size(TILE)
    devices = lax.axis_size(SLAB) * tiles
    plates, inlets = inlet_index.shape[2:]
    f32 = jnp.float32

    def both_ways(to_next, to_previous, axis):
        count = lax.axis_size(axis)
        forward = [(i, i + 1) for i in range(count - 1)]
        backward = [(target, source) for source, target in forward]
        return lax.ppermute(to_next, axis, forward), lax.ppermute(to_previous, axis, backward)

    own = lax.optimization_barrier(jnp.stack([right_side, diagonal]))
    before, after = both_ways(own[:, :, cy - HALO :], own[:, :, :HALO], TILE)
    own = jnp.concatenate([before, own, after], axis=2)
    low, high = both_ways(own, own, SLAB)

    hot, table, order, owner = pl.pallas_call(
        prepare_kernel,
        out_shape=(
            jax.ShapeDtypeStruct((plates * inlets + 8, LANES), f32),
            jax.ShapeDtypeStruct((plates * inlets // LANES, LANES), jnp.int32),
            jax.ShapeDtypeStruct((plates,), jnp.int32),
            jax.ShapeDtypeStruct((8, LANES), f32),
        ),
        in_specs=[pl.BlockSpec(memory_space=pltpu.HBM)] * 4,
        out_specs=(VMEM,) * 4,
        scratch_shapes=[
            pltpu.VMEM((inlets, plates), jnp.int32),
            pltpu.SMEM((OWNED,), f32),
            pltpu.SMEM((OWNED,), f32),
            pltpu.SemaphoreType.DMA((4,)),
        ],
        compiler_params=pltpu.CompilerParams(vmem_limit_bytes=4 * 1024 * 1024),
        cost_estimate=pl.CostEstimate(flops=800000, bytes_accessed=3200000, transcendentals=0),
        name="prepare",
    )(inlet_index[0, 0].T, plate_order, conductance, plate_level)

    wide = (3 * cz, cy + 2 * HALO, nx)
    tall = (wide[0], wide[1] + 2 * HALO, nx)
    cells = cz * cy
    copies = lax.axis_size("x")
    lines = tiles // (WIDTH * PACKED)
    payload, basis, last = pl.pallas_call(
        basis_kernel,
        out_shape=(
            jax.ShapeDtypeStruct((copies * WIDTH * (lines + 1), LANES), f32),
            jax.ShapeDtypeStruct((cells * FIELDS, nx), f32),
            jax.ShapeDtypeStruct((cells, nx), f32),
        ),
        in_specs=[VMEM] * 6,
        out_specs=(VMEM, VMEM, VMEM),
        scratch_shapes=[
            pltpu.VMEM(wide, f32),
            pltpu.VMEM(wide, f32),
            pltpu.VMEM(tall, f32),
            pltpu.VMEM(tall, f32),
            pltpu.VMEM((24 * 8, nx), f32),
            pltpu.VMEM((plates * FIELDS, nx), f32),
            pltpu.SMEM((plates * inlets,), jnp.int32),
            pltpu.SMEM((plates,), jnp.int32),
            pltpu.SemaphoreType.DMA((2,)),
        ],
        compiler_params=pltpu.CompilerParams(vmem_limit_bytes=8 * 1024 * 1024),
        name="basis",
    )(own, low, high, hot, table.reshape(plates * inlets), order)

    group = copies * WIDTH
    arrived = lax.all_to_all(
        payload.reshape(group * (lines + 1), 1, LANES), ("x", "y"), 0, 0, tiled=True
    )
    ends = lax.axis_size("core") * lax.axis_size("z")
    rows = pl.pallas_call(
        functools.partial(rows_kernel, lines=lines),
        out_shape=jax.ShapeDtypeStruct((ends, LANES), f32),
        in_specs=[VMEM],
        out_specs=VMEM,
        compiler_params=pltpu.CompilerParams(vmem_limit_bytes=2 * 1024 * 1024),
        name="rows",
    )(arrived.reshape(group * (lines + 1), LANES))
    arrived = lax.all_to_all(rows.reshape(ends, 1, LANES), ("core", "z"), 0, 0, tiled=True)
    scale = float(1.0 / (devices * inlets) ** 0.5)
    solution, residual, flow = pl.pallas_call(
        functools.partial(final_kernel, scale=scale),
        out_shape=(
            jax.ShapeDtypeStruct((cells, nx), f32),
            jax.ShapeDtypeStruct((cells, nx), f32),
            jax.ShapeDtypeStruct((OWNED,), f32),
        ),
        in_specs=[VMEM, VMEM, VMEM, VMEM],
        out_specs=(VMEM, VMEM, SMEM),
        compiler_params=pltpu.CompilerParams(vmem_limit_bytes=4 * 1024 * 1024),
        name="final",
    )(arrived.reshape(ends, LANES), basis, last, owner)
    return (solution.reshape(cz, cy, nx), residual.reshape(cz, cy, nx), flow)


def solution(mesh):
    slabs, tiles = mesh.devices.shape
    chips = mesh.devices.reshape(slabs // 2, 2, tiles // WIDTH, WIDTH)
    fine = jax.sharding.Mesh(chips, SLAB + TILE)
    in_specs = (
        P(SLAB, TILE, None),
        P(SLAB, TILE, None),
        P(SLAB, TILE, None, None),
        P(),
        P(TILE),
        P(TILE),
    )
    out_specs = (P(SLAB, TILE, None), P(SLAB, TILE, None), P(TILE))
    return jax.shard_map(
        on_device, mesh=fine, in_specs=in_specs, out_specs=out_specs, check_vma=False
    )
```

```python
import functools

import jax
import jax.numpy as jnp
from jax import lax
from jax.experimental import pallas as pl
from jax.experimental.pallas import tpu as pltpu
from jax.sharding import PartitionSpec as P

HALO = 8
DEGREE = 8
FIELDS = 8
OWNED = 4
WIDTH = 8
PACKED = 4
LANES = 128
HIGH_LANE = 48
LOW_LANE = 96
CENTER = 64
SLAB = ("x", "core")
TILE = ("z", "y")


def two_sum(a, b):
    s = a + b
    v = s - a
    return s, (a - (s - v)) + (b - v)


def quick_two_sum(a, b):
    s = a + b
    return s, b - (s - a)


def split(a):
    c = a * 4097.0
    high = c - (c - a)
    return high, a - high


def two_prod(a, b):
    p = a * b
    ah, al = split(a)
    bh, bl = split(b)
    return p, ((ah * bh - p) + ah * bl + al * bh) + al * bl


def dd_add(x, y):
    s, e = two_sum(x[0], y[0])
    t, f = two_sum(x[1], y[1])
    s, e = quick_two_sum(s, e + t)
    return quick_two_sum(s, e + f)


def dd_mul(x, y):
    p, e = two_prod(x[0], y[0])
    return quick_two_sum(p, e + (x[0] * y[1] + x[1] * y[0]))


def dd_scale(x, power):
    return x[0] * power, x[1] * power


def dd_neg(x):
    return -x[0], -x[1]


def dd_sum(terms):
    total = terms[0]
    for term in terms[1:]:
        total = dd_add(total, term)
    return total


def lane_of(shape):
    return lax.broadcasted_iota(jnp.int32, shape, len(shape) - 1)


def one_hot(found, dtype):
    return jnp.where(found, 1.0, 0.0).astype(dtype)


def prepare_kernel(index, order, conductance, level, lanes_hot, rows_hot, owner):
    inlets, plates = index.shape
    low = (index[...] & 127).astype(jnp.float32)
    high = (index[...] >> 7).astype(jnp.float32)
    both = jnp.concatenate([low, high], axis=0).astype(jnp.bfloat16)
    row = lax.broadcasted_iota(jnp.int32, (plates, plates), 0)
    column = lane_of((plates, plates))
    group = column // (PACKED * OWNED)
    line, y = group // WIDTH, group % WIDTH
    place, q = (column // OWNED) % PACKED, column % OWNED
    owned = ((line * PACKED + place) * WIDTH + y) * OWNED + q
    for choice in (row == order[...], row == owned):
        both = jnp.dot(both, one_hot(choice, jnp.bfloat16), preferred_element_type=jnp.float32)
        both = both.astype(jnp.bfloat16)
    cells = both.astype(jnp.float32).astype(jnp.int32)
    at = lax.broadcasted_iota(jnp.int32, (LANES, plates), 0)
    for slot in range(inlets):
        step, start = slot // 2, (slot % 2) * plates
        hot = one_hot(at == cells[slot : slot + 1], jnp.bfloat16)
        lanes_hot[step, :LANES, start : start + plates] = hot
        lanes_hot[step, LANES:, start : start + plates] = hot
        rows_hot[step, :, start : start + plates] = one_hot(
            at == cells[inlets + slot : inlets + slot + 1], jnp.float32
        )
    lane = lane_of((8, LANES))
    first = lax.broadcasted_iota(jnp.int32, (8, LANES), 0) == 0
    values = jnp.zeros((8, LANES), jnp.float32)
    for q in range(OWNED):
        values = jnp.where(lane == q * FIELDS, jnp.where(first, conductance[q], level[q]), values)
    owner[...] = values


def basis_kernel(
    own, low, high, lanes_hot, rows_hot, payload, basis,
    alpha, beta, even, odd, parts, halves, turned,
):
    cz = own.shape[1]
    wide_y = own.shape[2]
    cy = wide_y - 2 * HALO
    for place, source in enumerate((low, own, high)):
        at = pl.ds(place * cz, cz)
        even[at, HALO : HALO + wide_y, :] = source[0]
        diag = source[1]
        inside = jnp.where(diag > 0.0, 0.25, 0.0)
        beta[at] = inside
        alpha[at] = (diag - 1.0) * inside
    lane = lane_of((wide_y, LANES))
    planes = 3 * cz
    edge = jnp.zeros((planes, HALO, LANES), jnp.float32)
    for field in (even, odd):
        field[:, :HALO, :] = edge
        field[:, HALO + wide_y :, :] = edge
    rows = pl.ds(HALO, wide_y)
    inner = pl.ds(2 * HALO, cy)

    cells = cz * cy

    def emit(field, degree):
        for z in range(cz):
            value = field[cz + z, inner, :]
            at = pl.ds(degree * cells + z * cy, cy)
            basis[at, :] = value
            if degree < FIELDS:
                upper = value.astype(jnp.bfloat16)
                halves[at, :LANES] = upper
                halves[at, LANES:] = (value - upper.astype(jnp.float32)).astype(jnp.bfloat16)

    def product(first, second, slot):
        total = None
        for z in range(cz):
            term = first[cz + z, inner, :] * second[cz + z, inner, :]
            term = term[:8] + term[8:]
            total = term if total is None else total + term
        parts[pl.ds(slot * 8, 8), :] = total

    emit(even, 0)
    product(even, even, 0)
    now, later = even, odd
    for degree in range(DEGREE):

        def plane(z, now=now, later=later, degree=degree):
            value = now[z, rows, :]
            beside = now[z - 1, rows, :] + now[z + 1, rows, :]
            beside = beside + now[z, pl.ds(HALO - 1, wide_y), :] + now[z, pl.ds(HALO + 1, wide_y), :]
            beside = beside + jnp.where(lane == 0, 0.0, pltpu.roll(value, 1, 1))
            beside = beside + jnp.where(lane == LANES - 1, 0.0, pltpu.roll(value, LANES - 1, 1))
            fresh = alpha[z] * value - beta[z] * beside
            if degree == 0:
                later[z, rows, :] = 0.5 * fresh
            else:
                later[z, rows, :] = fresh - later[z, rows, :]

        for z in range(degree + 1, planes - 1 - degree):
            plane(z)
        emit(later, degree + 1)
        product(now, later, 2 * degree + 1)
        product(later, later, 2 * degree + 2)
        now, later = later, now

    slots = parts.shape[0] // 8
    for slot in range(2 * DEGREE + 1, slots):
        parts[pl.ds(slot * 8, 8), :] = jnp.zeros((8, LANES), jnp.float32)
    value = parts[pl.ds(0, slots, stride=8), :]
    error = jnp.zeros_like(value)
    for row in range(1, 8):
        value, extra = two_sum(value, parts[pl.ds(row, slots, stride=8), :])
        error = error + extra
    step = LANES // 2
    while step:
        value, extra = two_sum(value, pltpu.roll(value, step, 1))
        error = error + pltpu.roll(error, step, 1) + extra
        step //= 2
    lane_s = lane_of((slots, LANES))
    row_s = lax.broadcasted_iota(jnp.int32, (slots, LANES), 0)
    parity = row_s % 2 == 0
    base = jnp.where(parity, value[0:1], value[1:2])
    base_error = jnp.where(parity, error[0:1], error[1:2])
    value, extra = two_sum(2.0 * value, -base)
    error = (2.0 * error - base_error) + extra
    value, error = quick_two_sum(value, error)
    placed = jnp.where(jnp.abs(lane_s - HIGH_LANE) == row_s, value, 0.0)
    placed = placed + jnp.where(jnp.abs(lane_s - LOW_LANE) == row_s, error, 0.0)
    placed = jnp.where(row_s <= 2 * DEGREE, placed, 0.0)
    moments = jnp.sum(placed, axis=0, keepdims=True)

    steps, depth, columns = rows_hot.shape
    plates = columns // 2
    tile = 2 * LANES
    groups = plates // LANES

    totals = [jnp.zeros((FIELDS, 8, LANES), jnp.float32)] * groups
    for step in range(steps):
        for start in range(0, columns, tile):
            picked = jnp.dot(
                halves[...], lanes_hot[step, :, start : start + tile], preferred_element_type=jnp.float32
            )
            mask = rows_hot[step, :, start : start + tile].reshape(1, depth // 8, 8, tile)
            picked = jnp.sum(picked.reshape(FIELDS, depth // 8, 8, tile) * mask, axis=1)
            for side in range(2):
                group = (start // LANES + side) % groups
                totals[group] = totals[group] + picked[:, :, side * LANES : (side + 1) * LANES]
    for group, total in enumerate(totals):
        turned[pl.ds(group * LANES, LANES), :FIELDS] = jnp.sum(total, axis=1).T

    lines = plates // (OWNED * WIDTH * PACKED)
    rows_per = WIDTH * (lines + 1)
    sources = payload.shape[0] // rows_per
    packed = PACKED * OWNED
    lane_w = lane_of((lines * WIDTH, LANES))
    out = jnp.zeros((lines * WIDTH, LANES), jnp.float32)
    for at in range(packed):
        column = turned[pl.ds(at, lines * WIDTH, stride=packed), :]
        if at:
            column = pltpu.roll(column, at * FIELDS, 1)
        out = jnp.where(lane_w // FIELDS == at, column, out)
    for line in range(lines):
        for at in range(sources):
            payload[pl.ds(at * rows_per + line, WIDTH, stride=lines + 1), :] = out[line * WIDTH : (line + 1) * WIDTH]
    out = jnp.broadcast_to(moments, (WIDTH, LANES))
    for at in range(sources):
        payload[pl.ds(at * rows_per + lines, WIDTH, stride=lines + 1), :] = out


def with_error(value, error):
    lane = lane_of(value.shape)
    shifted = pltpu.roll(error, LOW_LANE - HIGH_LANE, 1)
    first = lane < OWNED * FIELDS
    return value + jnp.where(first, error, 0.0) + jnp.where(lane >= LOW_LANE - 2 * DEGREE, shifted, 0.0)


def sum_rows(rows, step):
    value = rows[pl.ds(0, 8), :]
    error = jnp.zeros_like(value)
    for at in range(8, rows.shape[0], 8):
        value, extra = two_sum(value, rows[pl.ds(at, 8), :])
        error = error + extra
    while step < 8:
        value, extra = two_sum(value, pltpu.roll(value, step, 0))
        error = error + pltpu.roll(error, step, 0) + extra
        step *= 2
    return value, error


def rows_kernel(rows, out, lines=1):
    value, error = sum_rows(rows, lines + 1)
    moments = with_error(value, error)[lines : lines + 1]
    total = value + error
    depth = lines * PACKED
    row = lax.broadcasted_iota(jnp.int32, (8, LANES), 0)
    first = lane_of((1, LANES)) < OWNED * FIELDS
    made = []
    for z in range(depth):
        line = total[z // PACKED : z // PACKED + 1]
        place = (z % PACKED) * OWNED * FIELDS
        if place:
            line = pltpu.roll(line, LANES - place, 1)
        made.append(jnp.where(first, line, moments))
    for at in range(0, out.shape[0], depth):
        for z in range(depth):
            out[pl.ds(at + z, 1), :] = made[z]


def shift(row, amount):
    return pltpu.roll(row, (-amount) % LANES, 1)


def apply_operator(coeffs):
    count = len(coeffs)
    terms = [[] for _ in range(count + 1)]
    for j, value in enumerate(coeffs):
        terms[j].append(dd_add(dd_scale(value, 8.0), dd_neg(value)))
        if j == 0:
            terms[1].append(dd_scale(value, 8.0))
        else:
            terms[j + 1].append(dd_scale(value, 4.0))
            terms[j - 1].append(dd_scale(value, 4.0))
    return [dd_sum(group) for group in terms]


def multiply(left, right):
    terms = [[] for _ in range(len(left) + len(right) - 1)]
    for i, a in enumerate(left):
        for j, b in enumerate(right):
            half = dd_scale(dd_mul(a, b), 0.5)
            terms[i + j].append(half)
            terms[abs(i - j)].append(half)
    return [dd_sum(group) for group in terms]


def square(values):
    terms = [[] for _ in range(2 * len(values) - 1)]
    for i, a in enumerate(values):
        for j in range(i, len(values)):
            term = dd_mul(a, values[j])
            if i == j:
                term = dd_scale(term, 0.5)
            terms[i + j].append(term)
            terms[j - i].append(term)
    return [dd_sum(group) for group in terms]


def galerkin(folded):
    high, low = folded
    moment = high + low
    beside = dd_add((shift(high, 1), shift(low, 1)), (shift(high, -1), shift(low, -1)))
    eight = dd_scale(folded, 8.0)
    weight = dd_add(dd_add(dd_scale(beside, 4.0), eight), dd_neg(folded))
    weight = weight[0] + weight[1]

    def entry(source, j):
        return jnp.broadcast_to(source[:, CENTER + j : CENTER + j + 1], source.shape)

    weights = [entry(weight, j) for j in range(7)]
    rhs = [entry(moment, j) for j in range(4)]
    matrix = [[0.5 * (weights[i + j] + weights[abs(i - j)]) for j in range(4)] for i in range(4)]
    inverse = []
    for k in range(4):
        inverse.append(1.0 / matrix[k][k])
        for i in range(k + 1, 4):
            factor = matrix[i][k] * inverse[k]
            for j in range(k + 1, i + 1):
                matrix[i][j] = matrix[i][j] - factor * matrix[j][k]
            rhs[i] = rhs[i] - factor * rhs[k]
    result = [None] * 4
    for i in range(3, -1, -1):
        value = rhs[i]
        for j in range(i + 1, 4):
            value = value - matrix[j][i] * result[j]
        result[i] = value * inverse[i]
    return result


def final_kernel(rows, basis, owner, solution, residual, flow, scale=1.0):
    row = with_error(*sum_rows(rows, 1))
    lane = lane_of((8, LANES))
    valid = jnp.abs(lane - CENTER) <= 2 * DEGREE
    high = jnp.where(valid, pltpu.roll(row, CENTER - HIGH_LANE, 1), 0.0)
    low = jnp.where(valid, pltpu.roll(row, LANES + CENTER - LOW_LANE, 1), 0.0)
    mu = quick_two_sum(high, low)
    zero = jnp.zeros((8, LANES), jnp.float32)
    first_coeffs = galerkin(mu)
    change = apply_operator([(value, zero) for value in first_coeffs])
    poly = [dd_neg(value) for value in change]
    poly[0] = dd_add(poly[0], (zero + 1.0, zero))
    nu = None
    for c, value in enumerate(square(poly)):
        if c == 0:
            overlap = mu
        else:
            up = (shift(mu[0], c), shift(mu[1], c))
            down = (shift(mu[0], -c), shift(mu[1], -c))
            overlap = dd_scale(dd_add(up, down), 0.5)
        term = dd_mul(value, overlap)
        nu = term if nu is None else dd_add(nu, term)
    second_coeffs = galerkin(nu)
    gain = multiply([(value, zero) for value in second_coeffs], poly)
    drop = apply_operator(gain)
    solved = list(gain)
    for j in range(4):
        solved[j] = dd_add(gain[j], (first_coeffs[j], zero))
    left = [dd_neg(value) for value in drop]
    for j in range(5):
        left[j] = dd_add(left[j], poly[j])
    solved = [value[0] + value[1] for value in solved]
    left = [value[0] + value[1] for value in left]

    cells = solution.shape[0]
    for at in range(0, cells, 8):
        fields = [basis[pl.ds(k * cells + at, 8), :] for k in range(DEGREE + 1)]
        total = solved[0] * fields[0]
        rest = left[0] * fields[0]
        for k in range(1, DEGREE + 1):
            if k < FIELDS:
                total = total + solved[k] * fields[k]
            rest = rest + left[k] * fields[k]
        solution[pl.ds(at, 8), :] = total
        residual[pl.ds(at, 8), :] = rest

    weights = zero
    for k in range(FIELDS):
        weights = jnp.where(lane % FIELDS == k, solved[k], weights)
    header = row * weights
    for step in (4, 2, 1):
        header = header + shift(header, step)
    result = owner[0:1, :] * (header[0:1, :] * scale - owner[1:2, :])
    for q in range(OWNED):
        flow[q] = result[0, q * FIELDS]


VMEM = pl.BlockSpec(memory_space=pltpu.VMEM)
SMEM = pl.BlockSpec(memory_space=pltpu.SMEM)


def on_device(right_side, diagonal, inlet_index, plate_order, conductance, plate_level):
    cz, cy, nx = right_side.shape
    tiles = lax.axis_size(TILE)
    devices = lax.axis_size(SLAB) * tiles
    plates, inlets = inlet_index.shape[2:]
    f32 = jnp.float32

    def both_ways(to_next, to_previous, axis):
        count = lax.axis_size(axis)
        forward = [(i, i + 1) for i in range(count - 1)]
        backward = [(target, source) for source, target in forward]
        return lax.ppermute(to_next, axis, forward), lax.ppermute(to_previous, axis, backward)

    own = lax.optimization_barrier(jnp.stack([right_side, diagonal]))
    before, after = both_ways(own[:, :, cy - HALO :], own[:, :, :HALO], TILE)
    own = jnp.concatenate([before, own, after], axis=2)
    low, high = both_ways(own, own, SLAB)

    lanes_hot, rows_hot, owner = pl.pallas_call(
        prepare_kernel,
        out_shape=(
            jax.ShapeDtypeStruct((inlets // 2, 2 * LANES, 2 * plates), jnp.bfloat16),
            jax.ShapeDtypeStruct((inlets // 2, LANES, 2 * plates), f32),
            jax.ShapeDtypeStruct((8, LANES), f32),
        ),
        in_specs=[VMEM, VMEM, SMEM, SMEM],
        out_specs=(VMEM,) * 3,
        compiler_params=pltpu.CompilerParams(vmem_limit_bytes=8 * 1024 * 1024),
        cost_estimate=pl.CostEstimate(flops=20000000, bytes_accessed=6400000, transcendentals=0),
        name="prepare",
    )(inlet_index[0, 0].T, plate_order.reshape(1, plates), conductance, plate_level)

    wide = (3 * cz, cy + 2 * HALO, nx)
    tall = (wide[0], wide[1] + 2 * HALO, nx)
    cells = cz * cy
    copies = lax.axis_size("x")
    lines = tiles // (WIDTH * PACKED)
    payload, basis = pl.pallas_call(
        basis_kernel,
        out_shape=(
            jax.ShapeDtypeStruct((copies * WIDTH * (lines + 1), LANES), f32),
            jax.ShapeDtypeStruct(((DEGREE + 1) * cells, nx), f32),
        ),
        in_specs=[VMEM] * 5,
        out_specs=(VMEM, VMEM),
        scratch_shapes=[
            pltpu.VMEM(wide, f32),
            pltpu.VMEM(wide, f32),
            pltpu.VMEM(tall, f32),
            pltpu.VMEM(tall, f32),
            pltpu.VMEM((24 * 8, nx), f32),
            pltpu.VMEM((FIELDS * cells, 2 * nx), jnp.bfloat16),
            pltpu.VMEM((plates, LANES), f32),
        ],
        compiler_params=pltpu.CompilerParams(vmem_limit_bytes=8 * 1024 * 1024),
        name="basis",
    )(own, low, high, lanes_hot, rows_hot)

    group = copies * WIDTH
    arrived = lax.all_to_all(
        payload.reshape(group * (lines + 1), 1, LANES), ("x", "y"), 0, 0, tiled=True
    )
    ends = lax.axis_size("core") * lax.axis_size("z")
    rows = pl.pallas_call(
        functools.partial(rows_kernel, lines=lines),
        out_shape=jax.ShapeDtypeStruct((ends, LANES), f32),
        in_specs=[VMEM],
        out_specs=VMEM,
        compiler_params=pltpu.CompilerParams(vmem_limit_bytes=2 * 1024 * 1024),
        name="rows",
    )(arrived.reshape(group * (lines + 1), LANES))
    arrived = lax.all_to_all(rows.reshape(ends, 1, LANES), ("core", "z"), 0, 0, tiled=True)
    scale = float(1.0 / (devices * inlets) ** 0.5)
    solution, residual, flow = pl.pallas_call(
        functools.partial(final_kernel, scale=scale),
        out_shape=(
            jax.ShapeDtypeStruct((cells, nx), f32),
            jax.ShapeDtypeStruct((cells, nx), f32),
            jax.ShapeDtypeStruct((OWNED,), f32),
        ),
        in_specs=[VMEM, VMEM, VMEM],
        out_specs=(VMEM, VMEM, SMEM),
        compiler_params=pltpu.CompilerParams(vmem_limit_bytes=4 * 1024 * 1024),
        name="final",
    )(arrived.reshape(ends, LANES), basis, owner)
    return (solution.reshape(cz, cy, nx), residual.reshape(cz, cy, nx), flow)


def solution(mesh):
    slabs, tiles = mesh.devices.shape
    chips = mesh.devices.reshape(slabs // 2, 2, tiles // WIDTH, WIDTH)
    fine = jax.sharding.Mesh(chips, SLAB + TILE)
    in_specs = (
        P(SLAB, TILE, None),
        P(SLAB, TILE, None),
        P(SLAB, TILE, None, None),
        P(),
        P(TILE),
        P(TILE),
    )
    out_specs = (P(SLAB, TILE, None), P(SLAB, TILE, None), P(TILE))
    return jax.shard_map(
        on_device, mesh=fine, in_specs=in_specs, out_specs=out_specs, check_vma=False
    )
```

```python
import functools

import jax
import jax.numpy as jnp
from jax import lax
from jax.experimental import pallas as pl
from jax.experimental.pallas import tpu as pltpu
from jax.sharding import PartitionSpec as P

HALO = 8
DEGREE = 8
FIELDS = 8
OWNED = 4
WIDTH = 8
PACKED = 4
LANES = 128
HIGH_LANE = 48
LOW_LANE = 96
CENTER = 64
SLAB = ("x", "core")
TILE = ("z", "y")


def two_sum(a, b):
    s = a + b
    v = s - a
    return s, (a - (s - v)) + (b - v)


def quick_two_sum(a, b):
    s = a + b
    return s, b - (s - a)


def split(a):
    c = a * 4097.0
    high = c - (c - a)
    return high, a - high


def two_prod(a, b):
    p = a * b
    ah, al = split(a)
    bh, bl = split(b)
    return p, ((ah * bh - p) + ah * bl + al * bh) + al * bl


def dd_add(x, y):
    s, e = two_sum(x[0], y[0])
    return quick_two_sum(s, e + (x[1] + y[1]))


def dd_mul(x, y):
    p, e = two_prod(x[0], y[0])
    return quick_two_sum(p, e + (x[0] * y[1] + x[1] * y[0]))


def dd_scale(x, power):
    return x[0] * power, x[1] * power


def dd_neg(x):
    return -x[0], -x[1]


def dd_sum(terms):
    terms = list(terms)
    while len(terms) > 1:
        terms = [dd_add(*terms[at : at + 2]) if at + 1 < len(terms) else terms[at] for at in range(0, len(terms), 2)]
    return terms[0]


def lane_of(shape):
    return lax.broadcasted_iota(jnp.int32, shape, len(shape) - 1)


def one_hot(found, dtype):
    return jnp.where(found, 1.0, 0.0).astype(dtype)


def prepare_kernel(packed, lanes_hot, rows_hot, owner):
    steps, _, columns = rows_hot.shape
    inlets, plates = 2 * steps, columns // 2
    index = packed[:inlets].astype(jnp.int32)
    order = packed[inlets : inlets + 1].astype(jnp.int32)
    low = (index & 127).astype(jnp.float32)
    high = (index >> 7).astype(jnp.float32)
    both = jnp.concatenate([low, high], axis=0).astype(jnp.bfloat16)
    row = lax.broadcasted_iota(jnp.int32, (plates, plates), 0)
    column = lane_of((plates, plates))
    group = column // (PACKED * OWNED)
    line, y = group // WIDTH, group % WIDTH
    place, q = (column // OWNED) % PACKED, column % OWNED
    owned = ((line * PACKED + place) * WIDTH + y) * OWNED + q
    for choice in (row == order, row == owned):
        both = jnp.dot(both, one_hot(choice, jnp.bfloat16), preferred_element_type=jnp.float32)
        both = both.astype(jnp.bfloat16)
    cells = both.astype(jnp.float32).astype(jnp.int32)
    at = lax.broadcasted_iota(jnp.int32, (LANES, plates), 0)
    for slot in range(inlets):
        step, start = slot // 2, (slot % 2) * plates
        hot = one_hot(at == cells[slot : slot + 1], jnp.bfloat16)
        lanes_hot[step, :LANES, start : start + plates] = hot
        lanes_hot[step, LANES:, start : start + plates] = hot
        rows_hot[step, :, start : start + plates] = one_hot(
            at == cells[inlets + slot : inlets + slot + 1], jnp.float32
        )
    lane = lane_of((8, LANES))
    first = lax.broadcasted_iota(jnp.int32, (8, LANES), 0) == 0
    values = jnp.zeros((8, LANES), jnp.float32)
    for q in range(OWNED):
        own, other = (packed[inlets + 1 : inlets + 2, at : at + 1] for at in (q, OWNED + q))
        values = jnp.where(lane == q * FIELDS, jnp.where(first, own, other), values)
    owner[...] = values


def basis_kernel(
    own, low, high, lanes_hot, rows_hot, payload, basis,
    alpha, beta, even, odd, parts, halves, turned,
):
    cz = own.shape[1]
    wide_y = own.shape[2]
    cy = wide_y - 2 * HALO
    for place, source in enumerate((low, own, high)):
        at = pl.ds(place * cz, cz)
        even[at, HALO : HALO + wide_y, :] = source[0]
        diag = source[1]
        inside = jnp.where(diag > 0.0, 0.25, 0.0)
        beta[at] = inside
        alpha[at] = (diag - 1.0) * inside
    lane = lane_of((wide_y, LANES))
    planes = 3 * cz
    edge = jnp.zeros((planes, HALO, LANES), jnp.float32)
    for field in (even, odd):
        field[:, :HALO, :] = edge
        field[:, HALO + wide_y :, :] = edge
    rows = pl.ds(HALO, wide_y)
    inner = pl.ds(2 * HALO, cy)

    cells = cz * cy

    def emit(field, degree):
        for z in range(cz):
            value = field[cz + z, inner, :]
            at = pl.ds(degree * cells + z * cy, cy)
            basis[at, :] = value
            if degree < FIELDS:
                upper = value.astype(jnp.bfloat16)
                halves[at, :LANES] = upper
                halves[at, LANES:] = (value - upper.astype(jnp.float32)).astype(jnp.bfloat16)

    def product(first, second, slot):
        total = None
        for z in range(cz):
            term = first[cz + z, inner, :] * second[cz + z, inner, :]
            term = term[:8] + term[8:]
            total = term if total is None else total + term
        parts[pl.ds(slot * 8, 8), :] = total

    emit(even, 0)
    product(even, even, 0)
    now, later = even, odd
    for degree in range(DEGREE):

        def plane(z, now=now, later=later, degree=degree):
            value = now[z, rows, :]
            beside = now[z - 1, rows, :] + now[z + 1, rows, :]
            beside = beside + now[z, pl.ds(HALO - 1, wide_y), :] + now[z, pl.ds(HALO + 1, wide_y), :]
            beside = beside + jnp.where(lane == 0, 0.0, pltpu.roll(value, 1, 1))
            beside = beside + jnp.where(lane == LANES - 1, 0.0, pltpu.roll(value, LANES - 1, 1))
            fresh = alpha[z] * value - beta[z] * beside
            if degree == 0:
                later[z, rows, :] = 0.5 * fresh
            else:
                later[z, rows, :] = fresh - later[z, rows, :]

        for z in range(degree + 1, planes - 1 - degree):
            plane(z)
        emit(later, degree + 1)
        product(now, later, 2 * degree + 1)
        product(later, later, 2 * degree + 2)
        now, later = later, now

    slots = parts.shape[0] // 8
    for slot in range(2 * DEGREE + 1, slots):
        parts[pl.ds(slot * 8, 8), :] = jnp.zeros((8, LANES), jnp.float32)
    value = parts[pl.ds(0, slots, stride=8), :]
    error = jnp.zeros_like(value)
    for row in range(1, 8):
        value, extra = two_sum(value, parts[pl.ds(row, slots, stride=8), :])
        error = error + extra
    step = LANES // 2
    while step:
        value, extra = two_sum(value, pltpu.roll(value, step, 1))
        error = error + pltpu.roll(error, step, 1) + extra
        step //= 2
    lane_s = lane_of((slots, LANES))
    row_s = lax.broadcasted_iota(jnp.int32, (slots, LANES), 0)
    parity = row_s % 2 == 0
    base = jnp.where(parity, value[0:1], value[1:2])
    base_error = jnp.where(parity, error[0:1], error[1:2])
    value, extra = two_sum(2.0 * value, -base)
    error = (2.0 * error - base_error) + extra
    value, error = quick_two_sum(value, error)
    placed = jnp.where(jnp.abs(lane_s - HIGH_LANE) == row_s, value, 0.0)
    placed = placed + jnp.where(jnp.abs(lane_s - LOW_LANE) == row_s, error, 0.0)
    placed = jnp.where(row_s <= 2 * DEGREE, placed, 0.0)
    moments = jnp.sum(placed, axis=0, keepdims=True)

    steps, depth, columns = rows_hot.shape
    plates = columns // 2
    tile = 2 * LANES
    groups = plates // LANES

    totals = [jnp.zeros((FIELDS, 8, LANES), jnp.float32)] * groups
    for step in range(steps):
        for start in range(0, columns, tile):
            picked = jnp.dot(
                halves[...], lanes_hot[step, :, start : start + tile], preferred_element_type=jnp.float32
            )
            mask = rows_hot[step, :, start : start + tile].reshape(1, depth // 8, 8, tile)
            picked = jnp.sum(picked.reshape(FIELDS, depth // 8, 8, tile) * mask, axis=1)
            for side in range(2):
                group = (start // LANES + side) % groups
                totals[group] = totals[group] + picked[:, :, side * LANES : (side + 1) * LANES]
    for group, total in enumerate(totals):
        turned[pl.ds(group * LANES, LANES), :FIELDS] = jnp.sum(total, axis=1).T

    lines = plates // (OWNED * WIDTH * PACKED)
    rows_per = WIDTH * (lines + 1)
    sources = payload.shape[0] // rows_per
    packed = PACKED * OWNED
    lane_w = lane_of((lines * WIDTH, LANES))
    out = jnp.zeros((lines * WIDTH, LANES), jnp.float32)
    for at in range(packed):
        column = turned[pl.ds(at, lines * WIDTH, stride=packed), :]
        if at:
            column = pltpu.roll(column, at * FIELDS, 1)
        out = jnp.where(lane_w // FIELDS == at, column, out)
    for line in range(lines):
        for at in range(sources):
            payload[pl.ds(at * rows_per + line, WIDTH, stride=lines + 1), :] = out[line * WIDTH : (line + 1) * WIDTH]
    out = jnp.broadcast_to(moments, (WIDTH, LANES))
    for at in range(sources):
        payload[pl.ds(at * rows_per + lines, WIDTH, stride=lines + 1), :] = out


def with_error(value, error):
    lane = lane_of(value.shape)
    shifted = pltpu.roll(error, LOW_LANE - HIGH_LANE, 1)
    first = lane < OWNED * FIELDS
    return value + jnp.where(first, error, 0.0) + jnp.where(lane >= LOW_LANE - 2 * DEGREE, shifted, 0.0)


def sum_rows(rows, step):
    value = rows[pl.ds(0, 8), :]
    error = jnp.zeros_like(value)
    for at in range(8, rows.shape[0], 8):
        value, extra = two_sum(value, rows[pl.ds(at, 8), :])
        error = error + extra
    while step < 8:
        value, extra = two_sum(value, pltpu.roll(value, step, 0))
        error = error + pltpu.roll(error, step, 0) + extra
        step *= 2
    return value, error


def rows_kernel(rows, out, lines=1):
    value, error = sum_rows(rows, lines + 1)
    moments = with_error(value, error)[lines : lines + 1]
    total = value + error
    depth = lines * PACKED
    row = lax.broadcasted_iota(jnp.int32, (8, LANES), 0)
    first = lane_of((1, LANES)) < OWNED * FIELDS
    made = []
    for z in range(depth):
        line = total[z // PACKED : z // PACKED + 1]
        place = (z % PACKED) * OWNED * FIELDS
        if place:
            line = pltpu.roll(line, LANES - place, 1)
        made.append(jnp.where(first, line, moments))
    for at in range(0, out.shape[0], depth):
        for z in range(depth):
            out[pl.ds(at + z, 1), :] = made[z]


def shift(row, amount):
    return pltpu.roll(row, (-amount) % LANES, 1)


def apply_operator(coeffs):
    count = len(coeffs)
    terms = [[] for _ in range(count + 1)]
    for j, value in enumerate(coeffs):
        terms[j].append(dd_add(dd_scale(value, 8.0), dd_neg(value)))
        if j == 0:
            terms[1].append(dd_scale(value, 8.0))
        else:
            terms[j + 1].append(dd_scale(value, 4.0))
            terms[j - 1].append(dd_scale(value, 4.0))
    return [dd_sum(group) for group in terms]


def multiply(left, right):
    terms = [[] for _ in range(len(left) + len(right) - 1)]
    for i, a in enumerate(left):
        for j, b in enumerate(right):
            half = dd_scale(dd_mul(a, b), 0.5)
            terms[i + j].append(half)
            terms[abs(i - j)].append(half)
    return [dd_sum(group) for group in terms]


def square(values):
    terms = [[] for _ in range(2 * len(values) - 1)]
    for i, a in enumerate(values):
        for j in range(i, len(values)):
            term = dd_mul(a, values[j])
            if i == j:
                term = dd_scale(term, 0.5)
            terms[i + j].append(term)
            terms[j - i].append(term)
    return [dd_sum(group) for group in terms]


def galerkin(folded):
    high, low = folded
    moment = high + low
    beside = dd_add((shift(high, 1), shift(low, 1)), (shift(high, -1), shift(low, -1)))
    eight = dd_scale(folded, 8.0)
    weight = dd_add(dd_add(dd_scale(beside, 4.0), eight), dd_neg(folded))
    weight = weight[0] + weight[1]

    def entry(source, j):
        return jnp.broadcast_to(source[:, CENTER + j : CENTER + j + 1], source.shape)

    weights = [entry(weight, j) for j in range(7)]
    rhs = [entry(moment, j) for j in range(4)]
    matrix = [[0.5 * (weights[i + j] + weights[abs(i - j)]) for j in range(4)] for i in range(4)]
    inverse = []
    for k in range(4):
        inverse.append(1.0 / matrix[k][k])
        for i in range(k + 1, 4):
            factor = matrix[i][k] * inverse[k]
            for j in range(k + 1, i + 1):
                matrix[i][j] = matrix[i][j] - factor * matrix[j][k]
            rhs[i] = rhs[i] - factor * rhs[k]
    result = [None] * 4
    for i in range(3, -1, -1):
        value = rhs[i]
        for j in range(i + 1, 4):
            value = value - matrix[j][i] * result[j]
        result[i] = value * inverse[i]
    return result


def final_kernel(rows, basis, owner, solution, residual, flow, scale=1.0):
    row = with_error(*sum_rows(rows, 1))
    lane = lane_of((8, LANES))
    valid = jnp.abs(lane - CENTER) <= 2 * DEGREE
    high = jnp.where(valid, pltpu.roll(row, CENTER - HIGH_LANE, 1), 0.0)
    low = jnp.where(valid, pltpu.roll(row, LANES + CENTER - LOW_LANE, 1), 0.0)
    mu = quick_two_sum(high, low)
    zero = jnp.zeros((8, LANES), jnp.float32)
    first_coeffs = galerkin(mu)
    change = apply_operator([(value, zero) for value in first_coeffs])
    poly = [dd_neg(value) for value in change]
    poly[0] = dd_add(poly[0], (zero + 1.0, zero))
    terms = []
    for c, value in enumerate(square(poly)):
        if c == 0:
            overlap = mu
        else:
            up = (shift(mu[0], c), shift(mu[1], c))
            down = (shift(mu[0], -c), shift(mu[1], -c))
            overlap = dd_scale(dd_add(up, down), 0.5)
        terms.append(dd_mul(value, overlap))
    nu = dd_sum(terms)
    second_coeffs = galerkin(nu)
    gain = multiply([(value, zero) for value in second_coeffs], poly)
    drop = apply_operator(gain)
    solved = list(gain)
    for j in range(4):
        solved[j] = dd_add(gain[j], (first_coeffs[j], zero))
    left = [dd_neg(value) for value in drop]
    for j in range(5):
        left[j] = dd_add(left[j], poly[j])
    solved = [value[0] + value[1] for value in solved]
    left = [value[0] + value[1] for value in left]

    cells = solution.shape[0]
    for at in range(0, cells, 8):
        fields = [basis[pl.ds(k * cells + at, 8), :] for k in range(DEGREE + 1)]
        total = solved[0] * fields[0]
        rest = left[0] * fields[0]
        for k in range(1, DEGREE + 1):
            if k < FIELDS:
                total = total + solved[k] * fields[k]
            rest = rest + left[k] * fields[k]
        solution[pl.ds(at, 8), :] = total
        residual[pl.ds(at, 8), :] = rest

    weights = zero
    for k in range(FIELDS):
        weights = jnp.where(lane % FIELDS == k, solved[k], weights)
    header = row * weights
    for step in (4, 2, 1):
        header = header + shift(header, step)
    result = owner[0:1, :] * (header[0:1, :] * scale - owner[1:2, :])
    for q in range(OWNED):
        flow[q] = result[0, q * FIELDS]


VMEM = pl.BlockSpec(memory_space=pltpu.VMEM)
SMEM = pl.BlockSpec(memory_space=pltpu.SMEM)


def on_device(right_side, diagonal, inlet_index, plate_order, conductance, plate_level):
    cz, cy, nx = right_side.shape
    tiles = lax.axis_size(TILE)
    devices = lax.axis_size(SLAB) * tiles
    plates, inlets = inlet_index.shape[2:]
    f32 = jnp.float32

    def both_ways(to_next, to_previous, axis):
        count = lax.axis_size(axis)
        forward = [(i, i + 1) for i in range(count - 1)]
        backward = [(target, source) for source, target in forward]
        return lax.ppermute(to_next, axis, forward), lax.ppermute(to_previous, axis, backward)

    own = lax.optimization_barrier(jnp.stack([right_side, diagonal]))
    before, after = both_ways(own[:, :, cy - HALO :], own[:, :, :HALO], TILE)
    own = jnp.concatenate([before, own, after], axis=2)
    low, high = both_ways(own, own, SLAB)

    owned = jnp.pad(jnp.concatenate([conductance, plate_level]), (0, plates - 2 * OWNED))
    packed = jnp.concatenate([inlet_index[0, 0].T.astype(f32), plate_order.astype(f32)[None], owned[None]])
    lanes_hot, rows_hot, owner = pl.pallas_call(
        prepare_kernel,
        out_shape=(
            jax.ShapeDtypeStruct((inlets // 2, 2 * LANES, 2 * plates), jnp.bfloat16),
            jax.ShapeDtypeStruct((inlets // 2, LANES, 2 * plates), f32),
            jax.ShapeDtypeStruct((8, LANES), f32),
        ),
        in_specs=[VMEM],
        out_specs=(VMEM,) * 3,
        compiler_params=pltpu.CompilerParams(vmem_limit_bytes=8 * 1024 * 1024),
        cost_estimate=pl.CostEstimate(flops=20000000, bytes_accessed=6400000, transcendentals=0),
        name="prepare",
    )(packed)

    wide = (3 * cz, cy + 2 * HALO, nx)
    tall = (wide[0], wide[1] + 2 * HALO, nx)
    cells = cz * cy
    copies = lax.axis_size("x")
    lines = tiles // (WIDTH * PACKED)
    payload, basis = pl.pallas_call(
        basis_kernel,
        out_shape=(
            jax.ShapeDtypeStruct((copies * WIDTH * (lines + 1), LANES), f32),
            jax.ShapeDtypeStruct(((DEGREE + 1) * cells, nx), f32),
        ),
        in_specs=[VMEM] * 5,
        out_specs=(VMEM, VMEM),
        scratch_shapes=[
            pltpu.VMEM(wide, f32),
            pltpu.VMEM(wide, f32),
            pltpu.VMEM(tall, f32),
            pltpu.VMEM(tall, f32),
            pltpu.VMEM((24 * 8, nx), f32),
            pltpu.VMEM((FIELDS * cells, 2 * nx), jnp.bfloat16),
            pltpu.VMEM((plates, LANES), f32),
        ],
        compiler_params=pltpu.CompilerParams(vmem_limit_bytes=8 * 1024 * 1024),
        name="basis",
    )(own, low, high, lanes_hot, rows_hot)

    group = copies * WIDTH
    arrived = lax.all_to_all(
        payload.reshape(group * (lines + 1), 1, LANES), ("x", "y"), 0, 0, tiled=True
    )
    ends = lax.axis_size("core") * lax.axis_size("z")
    rows = pl.pallas_call(
        functools.partial(rows_kernel, lines=lines),
        out_shape=jax.ShapeDtypeStruct((ends, LANES), f32),
        in_specs=[VMEM],
        out_specs=VMEM,
        compiler_params=pltpu.CompilerParams(vmem_limit_bytes=2 * 1024 * 1024),
        name="rows",
    )(arrived.reshape(group * (lines + 1), LANES))
    arrived = lax.all_to_all(rows.reshape(ends, 1, LANES), ("core", "z"), 0, 0, tiled=True)
    scale = float(1.0 / (devices * inlets) ** 0.5)
    solution, residual, flow = pl.pallas_call(
        functools.partial(final_kernel, scale=scale),
        out_shape=(
            jax.ShapeDtypeStruct((cells, nx), f32),
            jax.ShapeDtypeStruct((cells, nx), f32),
            jax.ShapeDtypeStruct((OWNED,), f32),
        ),
        in_specs=[VMEM, VMEM, VMEM],
        out_specs=(VMEM, VMEM, SMEM),
        compiler_params=pltpu.CompilerParams(vmem_limit_bytes=4 * 1024 * 1024),
        name="final",
    )(arrived.reshape(ends, LANES), basis, owner)
    return (solution.reshape(cz, cy, nx), residual.reshape(cz, cy, nx), flow)


def solution(mesh):
    slabs, tiles = mesh.devices.shape
    chips = mesh.devices.reshape(slabs // 2, 2, tiles // WIDTH, WIDTH)
    fine = jax.sharding.Mesh(chips, SLAB + TILE)
    in_specs = (
        P(SLAB, TILE, None),
        P(SLAB, TILE, None),
        P(SLAB, TILE, None, None),
        P(),
        P(TILE),
        P(TILE),
    )
    out_specs = (P(SLAB, TILE, None), P(SLAB, TILE, None), P(TILE))
    return jax.shard_map(
        on_device, mesh=fine, in_specs=in_specs, out_specs=out_specs, check_vma=False
    )
```

```python
import functools

import jax
import jax.numpy as jnp
from jax import lax
from jax.experimental import pallas as pl
from jax.experimental.pallas import tpu as pltpu
from jax.sharding import PartitionSpec as P

HALO = 8
DEGREE = 8
FIELDS = 8
OWNED = 4
WIDTH = 8
PACKED = 4
LANES = 128
HIGH_LANE = 48
LOW_LANE = 96
CENTER = 64
SLAB = ("x", "core")
TILE = ("z", "y")


def two_sum(a, b):
    s = a + b
    v = s - a
    return s, (a - (s - v)) + (b - v)


def quick_two_sum(a, b):
    s = a + b
    return s, b - (s - a)


def split(a):
    c = a * 4097.0
    high = c - (c - a)
    return high, a - high


def two_prod(a, b):
    p = a * b
    ah, al = split(a)
    bh, bl = split(b)
    return p, ((ah * bh - p) + ah * bl + al * bh) + al * bl


def dd_add(x, y):
    s, e = two_sum(x[0], y[0])
    return quick_two_sum(s, e + (x[1] + y[1]))


def dd_mul(x, y):
    p, e = two_prod(x[0], y[0])
    return quick_two_sum(p, e + (x[0] * y[1] + x[1] * y[0]))


def dd_scale(x, power):
    return x[0] * power, x[1] * power


def dd_neg(x):
    return -x[0], -x[1]


def dd_sum(terms):
    terms = list(terms)
    while len(terms) > 1:
        terms = [dd_add(*terms[at : at + 2]) if at + 1 < len(terms) else terms[at] for at in range(0, len(terms), 2)]
    return terms[0]


def lane_of(shape):
    return lax.broadcasted_iota(jnp.int32, shape, len(shape) - 1)


def one_hot(found, dtype):
    return jnp.where(found, 1.0, 0.0).astype(dtype)


def prepare_kernel(packed, lanes_hot, rows_hot, owner):
    steps, _, columns = rows_hot.shape
    inlets, plates = 2 * steps, columns // 2
    index = packed[:inlets].astype(jnp.int32)
    order = packed[inlets : inlets + 1].astype(jnp.int32)
    low = (index & 127).astype(jnp.float32)
    high = (index >> 7).astype(jnp.float32)
    both = jnp.concatenate([low, high], axis=0).astype(jnp.bfloat16)
    row = lax.broadcasted_iota(jnp.int32, (plates, plates), 0)
    column = lane_of((plates, plates))
    group = column // (PACKED * OWNED)
    line, y = group // WIDTH, group % WIDTH
    place, q = (column // OWNED) % PACKED, column % OWNED
    owned = ((line * PACKED + place) * WIDTH + y) * OWNED + q
    for choice in (row == order, row == owned):
        both = jnp.dot(both, one_hot(choice, jnp.bfloat16), preferred_element_type=jnp.float32)
        both = both.astype(jnp.bfloat16)
    cells = both.astype(jnp.float32).astype(jnp.int32)
    at = lax.broadcasted_iota(jnp.int32, (LANES, plates), 0)
    for slot in range(inlets):
        step, start = slot // 2, (slot % 2) * plates
        hot = one_hot(at == cells[slot : slot + 1], jnp.bfloat16)
        lanes_hot[step, :LANES, start : start + plates] = hot
        lanes_hot[step, LANES:, start : start + plates] = hot
        rows_hot[step, :, start : start + plates] = one_hot(
            at == cells[inlets + slot : inlets + slot + 1], jnp.float32
        )
    lane = lane_of((8, LANES))
    first = lax.broadcasted_iota(jnp.int32, (8, LANES), 0) == 0
    values = jnp.zeros((8, LANES), jnp.float32)
    for q in range(OWNED):
        own, other = (packed[inlets + 1 : inlets + 2, at : at + 1] for at in (q, OWNED + q))
        values = jnp.where(lane == q * FIELDS, jnp.where(first, own, other), values)
    owner[...] = values


def basis_kernel(
    own, low, high, lanes_hot, rows_hot, payload, basis,
    alpha, beta, even, odd, parts, halves, turned,
):
    cz = own.shape[1]
    wide_y = own.shape[2]
    cy = wide_y - 2 * HALO
    for place, source in enumerate((low, own, high)):
        at = pl.ds(place * cz, cz)
        even[at, HALO : HALO + wide_y, :] = source[0]
        diag = source[1]
        inside = jnp.where(diag > 0.0, 0.25, 0.0)
        beta[at] = inside
        alpha[at] = (diag - 1.0) * inside
    lane = lane_of((wide_y, LANES))
    planes = 3 * cz
    edge = jnp.zeros((planes, HALO, LANES), jnp.float32)
    for field in (even, odd):
        field[:, :HALO, :] = edge
        field[:, HALO + wide_y :, :] = edge
    rows = pl.ds(HALO, wide_y)
    inner = pl.ds(2 * HALO, cy)

    cells = cz * cy

    def emit(field, degree):
        for z in range(cz):
            value = field[cz + z, inner, :]
            at = pl.ds(degree * cells + z * cy, cy)
            basis[at, :] = value
            if degree < FIELDS:
                upper = value.astype(jnp.bfloat16)
                halves[at, :LANES] = upper
                halves[at, LANES:] = (value - upper.astype(jnp.float32)).astype(jnp.bfloat16)

    def product(first, second, slot):
        total = None
        for z in range(cz):
            term = first[cz + z, inner, :] * second[cz + z, inner, :]
            term = term[:8] + term[8:]
            total = term if total is None else total + term
        parts[pl.ds(slot * 8, 8), :] = total

    emit(even, 0)
    product(even, even, 0)
    now, later = even, odd
    for degree in range(DEGREE):

        def plane(z, now=now, later=later, degree=degree):
            value = now[z, rows, :]
            beside = now[z - 1, rows, :] + now[z + 1, rows, :]
            beside = beside + now[z, pl.ds(HALO - 1, wide_y), :] + now[z, pl.ds(HALO + 1, wide_y), :]
            beside = beside + jnp.where(lane == 0, 0.0, pltpu.roll(value, 1, 1))
            beside = beside + jnp.where(lane == LANES - 1, 0.0, pltpu.roll(value, LANES - 1, 1))
            fresh = alpha[z] * value - beta[z] * beside
            if degree == 0:
                later[z, rows, :] = 0.5 * fresh
            else:
                later[z, rows, :] = fresh - later[z, rows, :]

        for z in range(degree + 1, planes - 1 - degree):
            plane(z)
        emit(later, degree + 1)
        product(now, later, 2 * degree + 1)
        product(later, later, 2 * degree + 2)
        now, later = later, now

    slots = parts.shape[0] // 8
    for slot in range(2 * DEGREE + 1, slots):
        parts[pl.ds(slot * 8, 8), :] = jnp.zeros((8, LANES), jnp.float32)
    value = parts[pl.ds(0, slots, stride=8), :]
    error = jnp.zeros_like(value)
    for row in range(1, 8):
        value, extra = two_sum(value, parts[pl.ds(row, slots, stride=8), :])
        error = error + extra
    step = LANES // 2
    while step:
        value, extra = two_sum(value, pltpu.roll(value, step, 1))
        error = error + pltpu.roll(error, step, 1) + extra
        step //= 2
    lane_s = lane_of((slots, LANES))
    row_s = lax.broadcasted_iota(jnp.int32, (slots, LANES), 0)
    parity = row_s % 2 == 0
    base = jnp.where(parity, value[0:1], value[1:2])
    base_error = jnp.where(parity, error[0:1], error[1:2])
    value, extra = two_sum(2.0 * value, -base)
    error = (2.0 * error - base_error) + extra
    value, error = quick_two_sum(value, error)
    placed = jnp.where(jnp.abs(lane_s - HIGH_LANE) == row_s, value, 0.0)
    placed = placed + jnp.where(jnp.abs(lane_s - LOW_LANE) == row_s, error, 0.0)
    placed = jnp.where(row_s <= 2 * DEGREE, placed, 0.0)
    moments = jnp.sum(placed, axis=0, keepdims=True)

    steps, depth, columns = rows_hot.shape
    plates = columns // 2
    tile = 2 * LANES
    groups = plates // LANES

    totals = [jnp.zeros((FIELDS, 8, LANES), jnp.float32)] * groups
    for step in range(steps):
        for start in range(0, columns, tile):
            picked = jnp.dot(
                halves[...], lanes_hot[step, :, start : start + tile], preferred_element_type=jnp.float32
            )
            mask = rows_hot[step, :, start : start + tile].reshape(1, depth // 8, 8, tile)
            picked = jnp.sum(picked.reshape(FIELDS, depth // 8, 8, tile) * mask, axis=1)
            for side in range(2):
                group = (start // LANES + side) % groups
                totals[group] = totals[group] + picked[:, :, side * LANES : (side + 1) * LANES]
    for group, total in enumerate(totals):
        turned[pl.ds(group * LANES, LANES), :FIELDS] = jnp.sum(total, axis=1).T

    lines = plates // (OWNED * WIDTH * PACKED)
    rows_per = WIDTH * (lines + 1)
    sources = payload.shape[0] // rows_per
    packed = PACKED * OWNED
    lane_w = lane_of((lines * WIDTH, LANES))
    out = jnp.zeros((lines * WIDTH, LANES), jnp.float32)
    for at in range(packed):
        column = turned[pl.ds(at, lines * WIDTH, stride=packed), :]
        if at:
            column = pltpu.roll(column, at * FIELDS, 1)
        out = jnp.where(lane_w // FIELDS == at, column, out)
    for line in range(lines):
        for at in range(sources):
            payload[pl.ds(at * rows_per + line, WIDTH, stride=lines + 1), :] = out[line * WIDTH : (line + 1) * WIDTH]
    out = jnp.broadcast_to(moments, (WIDTH, LANES))
    for at in range(sources):
        payload[pl.ds(at * rows_per + lines, WIDTH, stride=lines + 1), :] = out


def with_error(value, error):
    lane = lane_of(value.shape)
    shifted = pltpu.roll(error, LOW_LANE - HIGH_LANE, 1)
    first = lane < OWNED * FIELDS
    return value + jnp.where(first, error, 0.0) + jnp.where(lane >= LOW_LANE - 2 * DEGREE, shifted, 0.0)


def sum_rows(rows, step):
    value = rows[pl.ds(0, 8), :]
    error = jnp.zeros_like(value)
    for at in range(8, rows.shape[0], 8):
        value, extra = two_sum(value, rows[pl.ds(at, 8), :])
        error = error + extra
    while step < 8:
        value, extra = two_sum(value, pltpu.roll(value, step, 0))
        error = error + pltpu.roll(error, step, 0) + extra
        step *= 2
    return value, error


def rows_kernel(rows, out, lines=1):
    value, error = sum_rows(rows, lines + 1)
    moments = with_error(value, error)[lines : lines + 1]
    total = value + error
    depth = lines * PACKED
    row = lax.broadcasted_iota(jnp.int32, (8, LANES), 0)
    first = lane_of((1, LANES)) < OWNED * FIELDS
    made = []
    for z in range(depth):
        line = total[z // PACKED : z // PACKED + 1]
        place = (z % PACKED) * OWNED * FIELDS
        if place:
            line = pltpu.roll(line, LANES - place, 1)
        made.append(jnp.where(first, line, moments))
    for at in range(0, out.shape[0], depth):
        for z in range(depth):
            out[pl.ds(at + z, 1), :] = made[z]


def shift(row, amount):
    return pltpu.roll(row, (-amount) % LANES, 1)


def apply_operator(coeffs):
    count = len(coeffs)
    terms = [[] for _ in range(count + 1)]
    for j, value in enumerate(coeffs):
        terms[j].append(dd_add(dd_scale(value, 8.0), dd_neg(value)))
        if j == 0:
            terms[1].append(dd_scale(value, 8.0))
        else:
            terms[j + 1].append(dd_scale(value, 4.0))
            terms[j - 1].append(dd_scale(value, 4.0))
    return [dd_sum(group) for group in terms]


def multiply(left, right):
    terms = [[] for _ in range(len(left) + len(right) - 1)]
    for i, a in enumerate(left):
        for j, b in enumerate(right):
            half = dd_scale(dd_mul(a, b), 0.5)
            terms[i + j].append(half)
            terms[abs(i - j)].append(half)
    return [dd_sum(group) for group in terms]


def square(values):
    terms = [[] for _ in range(2 * len(values) - 1)]
    for i, a in enumerate(values):
        for j in range(i, len(values)):
            term = dd_mul(a, values[j])
            if i == j:
                term = dd_scale(term, 0.5)
            terms[i + j].append(term)
            terms[j - i].append(term)
    return [dd_sum(group) for group in terms]


def galerkin(folded):
    high, low = folded
    moment = high + low
    beside = dd_add((shift(high, 1), shift(low, 1)), (shift(high, -1), shift(low, -1)))
    eight = dd_scale(folded, 8.0)
    weight = dd_add(dd_add(dd_scale(beside, 4.0), eight), dd_neg(folded))
    weight = weight[0] + weight[1]

    def entry(source, j):
        return jnp.broadcast_to(source[:, CENTER + j : CENTER + j + 1], source.shape)

    weights = [entry(weight, j) for j in range(7)]
    rhs = [entry(moment, j) for j in range(4)]
    matrix = [[0.5 * (weights[i + j] + weights[abs(i - j)]) for j in range(4)] for i in range(4)]
    inverse = []
    for k in range(4):
        inverse.append(1.0 / matrix[k][k])
        for i in range(k + 1, 4):
            factor = matrix[i][k] * inverse[k]
            for j in range(k + 1, i + 1):
                matrix[i][j] = matrix[i][j] - factor * matrix[j][k]
            rhs[i] = rhs[i] - factor * rhs[k]
    result = [None] * 4
    for i in range(3, -1, -1):
        value = rhs[i]
        for j in range(i + 1, 4):
            value = value - matrix[j][i] * result[j]
        result[i] = value * inverse[i]
    return result


def final_kernel(rows, basis, owner, solution, residual, flow, scale=1.0):
    row = with_error(*sum_rows(rows, 1))
    lane = lane_of((8, LANES))
    valid = jnp.abs(lane - CENTER) <= 2 * DEGREE
    high = jnp.where(valid, pltpu.roll(row, CENTER - HIGH_LANE, 1), 0.0)
    low = jnp.where(valid, pltpu.roll(row, LANES + CENTER - LOW_LANE, 1), 0.0)
    mu = quick_two_sum(high, low)
    zero = jnp.zeros((8, LANES), jnp.float32)
    first_coeffs = galerkin(mu)
    change = apply_operator([(value, zero) for value in first_coeffs])
    poly = [dd_neg(value) for value in change]
    poly[0] = dd_add(poly[0], (zero + 1.0, zero))
    terms = []
    for c, value in enumerate(square(poly)):
        if c == 0:
            overlap = mu
        else:
            up = (shift(mu[0], c), shift(mu[1], c))
            down = (shift(mu[0], -c), shift(mu[1], -c))
            overlap = dd_scale(dd_add(up, down), 0.5)
        terms.append(dd_mul(value, overlap))
    nu = dd_sum(terms)
    second_coeffs = galerkin(nu)
    gain = multiply([(value, zero) for value in second_coeffs], poly)
    drop = apply_operator(gain)
    solved = list(gain)
    for j in range(4):
        solved[j] = dd_add(gain[j], (first_coeffs[j], zero))
    left = [dd_neg(value) for value in drop]
    for j in range(5):
        left[j] = dd_add(left[j], poly[j])
    solved = [value[0] + value[1] for value in solved]
    left = [value[0] + value[1] for value in left]

    cells = solution.shape[0]
    for at in range(0, cells, 8):
        fields = [basis[pl.ds(k * cells + at, 8), :] for k in range(DEGREE + 1)]
        total = solved[0] * fields[0]
        rest = left[0] * fields[0]
        for k in range(1, DEGREE + 1):
            if k < FIELDS:
                total = total + solved[k] * fields[k]
            rest = rest + left[k] * fields[k]
        solution[pl.ds(at, 8), :] = total
        residual[pl.ds(at, 8), :] = rest

    weights = zero
    for k in range(FIELDS):
        weights = jnp.where(lane % FIELDS == k, solved[k], weights)
    header = row * weights
    for step in (4, 2, 1):
        header = header + shift(header, step)
    result = owner[0:1, :] * (header[0:1, :] * scale - owner[1:2, :])
    for q in range(OWNED):
        flow[q] = result[0, q * FIELDS]


VMEM = pl.BlockSpec(memory_space=pltpu.VMEM)
SMEM = pl.BlockSpec(memory_space=pltpu.SMEM)


def on_device(right_side, diagonal, inlet_index, plate_order, conductance, plate_level):
    cz, cy, nx = right_side.shape
    tiles = lax.axis_size(TILE)
    devices = lax.axis_size(SLAB) * tiles
    plates, inlets = inlet_index.shape[2:]
    f32 = jnp.float32

    def both_ways(to_next, to_previous, axis):
        count = lax.axis_size(axis)
        even = lax.axis_index(axis) % 2 == 0

        def swap(value, start):
            pairs = [(i, i + 1) for i in range(start, count - 1, 2)]
            return lax.ppermute(value, axis, pairs + [(target, source) for source, target in pairs])

        if to_next is to_previous:
            outer, inner = swap(to_next, 1), swap(to_next, 0)
        else:
            outer = swap(jnp.where(even, to_previous, to_next), 1)
            inner = swap(jnp.where(even, to_next, to_previous), 0)
        return jnp.where(even, outer, inner), jnp.where(even, inner, outer)

    own = lax.optimization_barrier(jnp.stack([right_side, diagonal]))
    before, after = both_ways(own[:, :, cy - HALO :], own[:, :, :HALO], TILE)
    own = jnp.concatenate([before, own, after], axis=2)
    low, high = both_ways(own, own, SLAB)

    owned = jnp.pad(jnp.concatenate([conductance, plate_level]), (0, plates - 2 * OWNED))
    packed = jnp.concatenate([inlet_index[0, 0].T.astype(f32), plate_order.astype(f32)[None], owned[None]])
    lanes_hot, rows_hot, owner = pl.pallas_call(
        prepare_kernel,
        out_shape=(
            jax.ShapeDtypeStruct((inlets // 2, 2 * LANES, 2 * plates), jnp.bfloat16),
            jax.ShapeDtypeStruct((inlets // 2, LANES, 2 * plates), f32),
            jax.ShapeDtypeStruct((8, LANES), f32),
        ),
        in_specs=[VMEM],
        out_specs=(VMEM,) * 3,
        compiler_params=pltpu.CompilerParams(vmem_limit_bytes=8 * 1024 * 1024),
        cost_estimate=pl.CostEstimate(flops=20000000, bytes_accessed=6400000, transcendentals=0),
        name="prepare",
    )(packed)

    wide = (3 * cz, cy + 2 * HALO, nx)
    tall = (wide[0], wide[1] + 2 * HALO, nx)
    cells = cz * cy
    copies = lax.axis_size("x")
    lines = tiles // (WIDTH * PACKED)
    payload, basis = pl.pallas_call(
        basis_kernel,
        out_shape=(
            jax.ShapeDtypeStruct((copies * WIDTH * (lines + 1), LANES), f32),
            jax.ShapeDtypeStruct(((DEGREE + 1) * cells, nx), f32),
        ),
        in_specs=[VMEM] * 5,
        out_specs=(VMEM, VMEM),
        scratch_shapes=[
            pltpu.VMEM(wide, f32),
            pltpu.VMEM(wide, f32),
            pltpu.VMEM(tall, f32),
            pltpu.VMEM(tall, f32),
            pltpu.VMEM((24 * 8, nx), f32),
            pltpu.VMEM((FIELDS * cells, 2 * nx), jnp.bfloat16),
            pltpu.VMEM((plates, LANES), f32),
        ],
        compiler_params=pltpu.CompilerParams(vmem_limit_bytes=8 * 1024 * 1024),
        name="basis",
    )(own, low, high, lanes_hot, rows_hot)

    group = copies * WIDTH
    arrived = lax.all_to_all(
        payload.reshape(group * (lines + 1), 1, LANES), ("x", "y"), 0, 0, tiled=True
    )
    ends = lax.axis_size("core") * lax.axis_size("z")
    rows = pl.pallas_call(
        functools.partial(rows_kernel, lines=lines),
        out_shape=jax.ShapeDtypeStruct((ends, LANES), f32),
        in_specs=[VMEM],
        out_specs=VMEM,
        compiler_params=pltpu.CompilerParams(vmem_limit_bytes=2 * 1024 * 1024),
        name="rows",
    )(arrived.reshape(group * (lines + 1), LANES))
    arrived = lax.all_to_all(rows.reshape(ends, 1, LANES), ("core", "z"), 0, 0, tiled=True)
    scale = float(1.0 / (devices * inlets) ** 0.5)
    solution, residual, flow = pl.pallas_call(
        functools.partial(final_kernel, scale=scale),
        out_shape=(
            jax.ShapeDtypeStruct((cells, nx), f32),
            jax.ShapeDtypeStruct((cells, nx), f32),
            jax.ShapeDtypeStruct((OWNED,), f32),
        ),
        in_specs=[VMEM, VMEM, VMEM],
        out_specs=(VMEM, VMEM, SMEM),
        compiler_params=pltpu.CompilerParams(vmem_limit_bytes=4 * 1024 * 1024),
        name="final",
    )(arrived.reshape(ends, LANES), basis, owner)
    return (solution.reshape(cz, cy, nx), residual.reshape(cz, cy, nx), flow)


def solution(mesh):
    slabs, tiles = mesh.devices.shape
    chips = mesh.devices.reshape(slabs // 2, 2, tiles // WIDTH, WIDTH)
    fine = jax.sharding.Mesh(chips, SLAB + TILE)
    in_specs = (
        P(SLAB, TILE, None),
        P(SLAB, TILE, None),
        P(SLAB, TILE, None, None),
        P(),
        P(TILE),
        P(TILE),
    )
    out_specs = (P(SLAB, TILE, None), P(SLAB, TILE, None), P(TILE))
    return jax.shard_map(
        on_device, mesh=fine, in_specs=in_specs, out_specs=out_specs, check_vma=False
    )
```

```python
import functools

import jax
import jax.numpy as jnp
from jax import lax
from jax.experimental import pallas as pl
from jax.experimental.pallas import tpu as pltpu
from jax.sharding import PartitionSpec as P

HALO = 8
DEGREE = 8
FIELDS = 8
OWNED = 4
WIDTH = 8
PACKED = 4
LANES = 128
HIGH_LANE = 48
LOW_LANE = 96
CENTER = 64
SLAB = ("x", "core")
TILE = ("z", "y")


def two_sum(a, b):
    s = a + b
    v = s - a
    return s, (a - (s - v)) + (b - v)


def quick_two_sum(a, b):
    s = a + b
    return s, b - (s - a)


def split(a):
    c = a * 4097.0
    high = c - (c - a)
    return high, a - high


def two_prod(a, b):
    p = a * b
    ah, al = split(a)
    bh, bl = split(b)
    return p, ((ah * bh - p) + ah * bl + al * bh) + al * bl


def dd_add(x, y):
    s, e = two_sum(x[0], y[0])
    return quick_two_sum(s, e + (x[1] + y[1]))


def dd_mul(x, y):
    p, e = two_prod(x[0], y[0])
    return quick_two_sum(p, e + (x[0] * y[1] + x[1] * y[0]))


def dd_scale(x, power):
    return x[0] * power, x[1] * power


def dd_neg(x):
    return -x[0], -x[1]


def dd_sum(terms):
    terms = list(terms)
    while len(terms) > 1:
        terms = [dd_add(*terms[at : at + 2]) if at + 1 < len(terms) else terms[at] for at in range(0, len(terms), 2)]
    return terms[0]


def lane_of(shape):
    return lax.broadcasted_iota(jnp.int32, shape, len(shape) - 1)


def one_hot(found, dtype):
    return jnp.where(found, 1.0, 0.0).astype(dtype)


def prepare_kernel(packed, lanes_hot, rows_hot, owner):
    steps, _, columns = rows_hot.shape
    inlets, plates = 2 * steps, columns // 2
    index = packed[:inlets].astype(jnp.int32)
    order = packed[inlets : inlets + 1].astype(jnp.int32)
    low = (index & 127).astype(jnp.float32)
    high = (index >> 7).astype(jnp.float32)
    both = jnp.concatenate([low, high], axis=0).astype(jnp.bfloat16)
    row = lax.broadcasted_iota(jnp.int32, (plates, plates), 0)
    column = lane_of((plates, plates))
    group = column // (PACKED * OWNED)
    line, y = group // WIDTH, group % WIDTH
    place, q = (column // OWNED) % PACKED, column % OWNED
    owned = ((line * PACKED + place) * WIDTH + y) * OWNED + q
    for choice in (row == order, row == owned):
        both = jnp.dot(both, one_hot(choice, jnp.bfloat16), preferred_element_type=jnp.float32)
        both = both.astype(jnp.bfloat16)
    cells = both.astype(jnp.float32).astype(jnp.int32)
    at = lax.broadcasted_iota(jnp.int32, (LANES, plates), 0)
    for slot in range(inlets):
        step, start = slot // 2, (slot % 2) * plates
        hot = one_hot(at == cells[slot : slot + 1], jnp.bfloat16)
        lanes_hot[step, :LANES, start : start + plates] = hot
        lanes_hot[step, LANES:, start : start + plates] = hot
        rows_hot[step, :, start : start + plates] = one_hot(
            at == cells[inlets + slot : inlets + slot + 1], jnp.float32
        )
    lane = lane_of((8, LANES))
    first = lax.broadcasted_iota(jnp.int32, (8, LANES), 0) == 0
    values = jnp.zeros((8, LANES), jnp.float32)
    for q in range(OWNED):
        own, other = (packed[inlets + 1 : inlets + 2, at : at + 1] for at in (q, OWNED + q))
        values = jnp.where(lane == q * FIELDS, jnp.where(first, own, other), values)
    owner[...] = values


def basis_kernel(
    own, low, high, lanes_hot, rows_hot, payload, basis,
    alpha, beta, even, odd, parts, halves, turned,
):
    cz = own.shape[1]
    wide_y = own.shape[2]
    cy = wide_y - 2 * HALO
    for place, source in enumerate((low, own, high)):
        at = pl.ds(place * cz, cz)
        even[at, HALO : HALO + wide_y, :] = source[0]
        diag = source[1]
        inside = jnp.where(diag > 0.0, 0.25, 0.0)
        beta[at] = inside
        alpha[at] = (diag - 1.0) * inside
    lane = lane_of((wide_y, LANES))
    planes = 3 * cz
    edge = jnp.zeros((planes, HALO, LANES), jnp.float32)
    for field in (even, odd):
        field[:, :HALO, :] = edge
        field[:, HALO + wide_y :, :] = edge
    rows = pl.ds(HALO, wide_y)
    inner = pl.ds(2 * HALO, cy)

    cells = cz * cy

    def emit(field, degree):
        for z in range(cz):
            value = field[cz + z, inner, :]
            at = pl.ds(degree * cells + z * cy, cy)
            basis[at, :] = value
            if degree < FIELDS:
                upper = value.astype(jnp.bfloat16)
                halves[at, :LANES] = upper
                halves[at, LANES:] = (value - upper.astype(jnp.float32)).astype(jnp.bfloat16)

    def product(first, second, slot):
        total = None
        for z in range(cz):
            term = first[cz + z, inner, :] * second[cz + z, inner, :]
            term = term[:8] + term[8:]
            total = term if total is None else total + term
        parts[pl.ds(slot * 8, 8), :] = total

    emit(even, 0)
    product(even, even, 0)
    now, later = even, odd
    for degree in range(DEGREE):

        def plane(z, now=now, later=later, degree=degree):
            value = now[z, rows, :]
            beside = now[z - 1, rows, :] + now[z + 1, rows, :]
            beside = beside + now[z, pl.ds(HALO - 1, wide_y), :] + now[z, pl.ds(HALO + 1, wide_y), :]
            beside = beside + jnp.where(lane == 0, 0.0, pltpu.roll(value, 1, 1))
            beside = beside + jnp.where(lane == LANES - 1, 0.0, pltpu.roll(value, LANES - 1, 1))
            fresh = alpha[z] * value - beta[z] * beside
            if degree == 0:
                later[z, rows, :] = 0.5 * fresh
            else:
                later[z, rows, :] = fresh - later[z, rows, :]

        for z in range(degree + 1, planes - 1 - degree):
            plane(z)
        emit(later, degree + 1)
        product(now, later, 2 * degree + 1)
        product(later, later, 2 * degree + 2)
        now, later = later, now

    slots = parts.shape[0] // 8
    for slot in range(2 * DEGREE + 1, slots):
        parts[pl.ds(slot * 8, 8), :] = jnp.zeros((8, LANES), jnp.float32)
    value = parts[pl.ds(0, slots, stride=8), :]
    error = jnp.zeros_like(value)
    for row in range(1, 8):
        value, extra = two_sum(value, parts[pl.ds(row, slots, stride=8), :])
        error = error + extra
    step = LANES // 2
    while step:
        value, extra = two_sum(value, pltpu.roll(value, step, 1))
        error = error + pltpu.roll(error, step, 1) + extra
        step //= 2
    lane_s = lane_of((slots, LANES))
    row_s = lax.broadcasted_iota(jnp.int32, (slots, LANES), 0)
    parity = row_s % 2 == 0
    base = jnp.where(parity, value[0:1], value[1:2])
    base_error = jnp.where(parity, error[0:1], error[1:2])
    value, extra = two_sum(2.0 * value, -base)
    error = (2.0 * error - base_error) + extra
    value, error = quick_two_sum(value, error)
    placed = jnp.where(jnp.abs(lane_s - HIGH_LANE) == row_s, value, 0.0)
    placed = placed + jnp.where(jnp.abs(lane_s - LOW_LANE) == row_s, error, 0.0)
    placed = jnp.where(row_s <= 2 * DEGREE, placed, 0.0)
    moments = jnp.sum(placed, axis=0, keepdims=True)

    steps, depth, columns = rows_hot.shape
    plates = columns // 2
    tile = 2 * LANES
    groups = plates // LANES

    totals = [jnp.zeros((FIELDS, 8, LANES), jnp.float32)] * groups
    for step in range(steps):
        for start in range(0, columns, tile):
            picked = jnp.dot(
                halves[...], lanes_hot[step, :, start : start + tile], preferred_element_type=jnp.float32
            )
            mask = rows_hot[step, :, start : start + tile].reshape(1, depth // 8, 8, tile)
            picked = jnp.sum(picked.reshape(FIELDS, depth // 8, 8, tile) * mask, axis=1)
            for side in range(2):
                group = (start // LANES + side) % groups
                totals[group] = totals[group] + picked[:, :, side * LANES : (side + 1) * LANES]
    for group, total in enumerate(totals):
        turned[pl.ds(group * LANES, LANES), :FIELDS] = jnp.sum(total, axis=1).T

    lines = plates // (OWNED * WIDTH * PACKED)
    rows_per = WIDTH * (lines + 1)
    sources = payload.shape[0] // rows_per
    packed = PACKED * OWNED
    lane_w = lane_of((lines * WIDTH, LANES))
    out = jnp.zeros((lines * WIDTH, LANES), jnp.float32)
    for at in range(packed):
        column = turned[pl.ds(at, lines * WIDTH, stride=packed), :]
        if at:
            column = pltpu.roll(column, at * FIELDS, 1)
        out = jnp.where(lane_w // FIELDS == at, column, out)
    for line in range(lines):
        for at in range(sources):
            payload[pl.ds(at * rows_per + line, WIDTH, stride=lines + 1), :] = out[line * WIDTH : (line + 1) * WIDTH]
    out = jnp.broadcast_to(moments, (WIDTH, LANES))
    for at in range(sources):
        payload[pl.ds(at * rows_per + lines, WIDTH, stride=lines + 1), :] = out


def with_error(value, error):
    lane = lane_of(value.shape)
    shifted = pltpu.roll(error, LOW_LANE - HIGH_LANE, 1)
    first = lane < OWNED * FIELDS
    return value + jnp.where(first, error, 0.0) + jnp.where(lane >= LOW_LANE - 2 * DEGREE, shifted, 0.0)


def sum_rows(rows, step):
    value = rows[pl.ds(0, 8), :]
    error = jnp.zeros_like(value)
    for at in range(8, rows.shape[0], 8):
        value, extra = two_sum(value, rows[pl.ds(at, 8), :])
        error = error + extra
    while step < 8:
        value, extra = two_sum(value, pltpu.roll(value, step, 0))
        error = error + pltpu.roll(error, step, 0) + extra
        step *= 2
    return value, error


def rows_kernel(rows, out, lines=1):
    value, error = sum_rows(rows, lines + 1)
    moments = with_error(value, error)[lines : lines + 1]
    total = value + error
    depth = lines * PACKED
    row = lax.broadcasted_iota(jnp.int32, (8, LANES), 0)
    first = lane_of((1, LANES)) < OWNED * FIELDS
    made = []
    for z in range(depth):
        line = total[z // PACKED : z // PACKED + 1]
        place = (z % PACKED) * OWNED * FIELDS
        if place:
            line = pltpu.roll(line, LANES - place, 1)
        made.append(jnp.where(first, line, moments))
    for at in range(0, out.shape[0], depth):
        for z in range(depth):
            out[pl.ds(at + z, 1), :] = made[z]


def shift(row, amount):
    return pltpu.roll(row, (-amount) % LANES, 1)


def apply_operator(coeffs):
    count = len(coeffs)
    terms = [[] for _ in range(count + 1)]
    for j, value in enumerate(coeffs):
        terms[j].append(dd_add(dd_scale(value, 8.0), dd_neg(value)))
        if j == 0:
            terms[1].append(dd_scale(value, 8.0))
        else:
            terms[j + 1].append(dd_scale(value, 4.0))
            terms[j - 1].append(dd_scale(value, 4.0))
    return [dd_sum(group) for group in terms]


def multiply(left, right):
    terms = [[] for _ in range(len(left) + len(right) - 1)]
    for i, a in enumerate(left):
        for j, b in enumerate(right):
            half = dd_scale(dd_mul(a, b), 0.5)
            terms[i + j].append(half)
            terms[abs(i - j)].append(half)
    return [dd_sum(group) for group in terms]


def square(values):
    terms = [[] for _ in range(2 * len(values) - 1)]
    for i, a in enumerate(values):
        for j in range(i, len(values)):
            term = dd_mul(a, values[j])
            if i == j:
                term = dd_scale(term, 0.5)
            terms[i + j].append(term)
            terms[j - i].append(term)
    return [dd_sum(group) for group in terms]


def galerkin(folded):
    high, low = folded
    moment = high + low
    beside = dd_add((shift(high, 1), shift(low, 1)), (shift(high, -1), shift(low, -1)))
    eight = dd_scale(folded, 8.0)
    weight = dd_add(dd_add(dd_scale(beside, 4.0), eight), dd_neg(folded))
    weight = weight[0] + weight[1]

    def entry(source, j):
        return jnp.broadcast_to(source[:, CENTER + j : CENTER + j + 1], source.shape)

    weights = [entry(weight, j) for j in range(7)]
    rhs = [entry(moment, j) for j in range(4)]
    matrix = [[0.5 * (weights[i + j] + weights[abs(i - j)]) for j in range(4)] for i in range(4)]
    inverse = []
    for k in range(4):
        inverse.append(1.0 / matrix[k][k])
        for i in range(k + 1, 4):
            factor = matrix[i][k] * inverse[k]
            for j in range(k + 1, i + 1):
                matrix[i][j] = matrix[i][j] - factor * matrix[j][k]
            rhs[i] = rhs[i] - factor * rhs[k]
    result = [None] * 4
    for i in range(3, -1, -1):
        value = rhs[i]
        for j in range(i + 1, 4):
            value = value - matrix[j][i] * result[j]
        result[i] = value * inverse[i]
    return result


def final_kernel(rows, basis, owner, solution, residual, flow, scale=1.0):
    row = with_error(*sum_rows(rows, 1))
    lane = lane_of((8, LANES))
    valid = jnp.abs(lane - CENTER) <= 2 * DEGREE
    high = jnp.where(valid, pltpu.roll(row, CENTER - HIGH_LANE, 1), 0.0)
    low = jnp.where(valid, pltpu.roll(row, LANES + CENTER - LOW_LANE, 1), 0.0)
    mu = quick_two_sum(high, low)
    zero = jnp.zeros((8, LANES), jnp.float32)
    first_coeffs = galerkin(mu)
    change = apply_operator([(value, zero) for value in first_coeffs])
    poly = [dd_neg(value) for value in change]
    poly[0] = dd_add(poly[0], (zero + 1.0, zero))
    terms = []
    for c, value in enumerate(square(poly)):
        if c == 0:
            overlap = mu
        else:
            up = (shift(mu[0], c), shift(mu[1], c))
            down = (shift(mu[0], -c), shift(mu[1], -c))
            overlap = dd_scale(dd_add(up, down), 0.5)
        terms.append(dd_mul(value, overlap))
    nu = dd_sum(terms)
    second_coeffs = galerkin(nu)
    gain = multiply([(value, zero) for value in second_coeffs], poly)
    drop = apply_operator(gain)
    solved = list(gain)
    for j in range(4):
        solved[j] = dd_add(gain[j], (first_coeffs[j], zero))
    left = [dd_neg(value) for value in drop]
    for j in range(5):
        left[j] = dd_add(left[j], poly[j])
    solved = [value[0] + value[1] for value in solved]
    left = [value[0] + value[1] for value in left]

    cells = solution.shape[0]
    for at in range(0, cells, 8):
        fields = [basis[pl.ds(k * cells + at, 8), :] for k in range(DEGREE + 1)]
        total = solved[0] * fields[0]
        rest = left[0] * fields[0]
        for k in range(1, DEGREE + 1):
            if k < FIELDS:
                total = total + solved[k] * fields[k]
            rest = rest + left[k] * fields[k]
        solution[pl.ds(at, 8), :] = total
        residual[pl.ds(at, 8), :] = rest

    weights = zero
    for k in range(FIELDS):
        weights = jnp.where(lane % FIELDS == k, solved[k], weights)
    header = row * weights
    for step in (4, 2, 1):
        header = header + shift(header, step)
    result = owner[0:1, :] * (header[0:1, :] * scale - owner[1:2, :])
    for q in range(OWNED):
        flow[q] = result[0, q * FIELDS]


VMEM = pl.BlockSpec(memory_space=pltpu.VMEM)
SMEM = pl.BlockSpec(memory_space=pltpu.SMEM)


def on_device(right_side, diagonal, inlet_index, plate_order, conductance, plate_level):
    cz, cy, nx = right_side.shape
    tiles = lax.axis_size(TILE)
    devices = lax.axis_size(SLAB) * tiles
    plates, inlets = inlet_index.shape[2:]
    f32 = jnp.float32

    def swap(value, axis, start):
        pairs = [(i, i + 1) for i in range(start, lax.axis_size(axis) - 1, 2)]
        return lax.ppermute(value, axis, pairs + [(target, source) for source, target in pairs])

    own = lax.optimization_barrier(jnp.stack([right_side, diagonal]))
    even = lax.axis_index(TILE) % 2 == 0
    first, last = own[:, :, :HALO], own[:, :, cy - HALO :]
    outer = swap(jnp.where(even, first, last), TILE, 1)
    inner = swap(jnp.where(even, last, first), TILE, 0)
    before, after = jnp.where(even, outer, inner), jnp.where(even, inner, outer)
    own = jnp.concatenate([before, own, after], axis=2)
    owned = jnp.pad(jnp.concatenate([conductance, plate_level]), (0, plates - 2 * OWNED))
    packed = jnp.concatenate([inlet_index[0, 0].T.astype(f32), plate_order.astype(f32)[None], owned[None]])
    outer, inner = swap(own, SLAB, 1), swap(own, SLAB, 0)
    odd = lax.axis_index(SLAB) % 2 == 1
    low, high = jnp.where(odd, inner, outer), jnp.where(odd, outer, inner)

    lanes_hot, rows_hot, owner = pl.pallas_call(
        prepare_kernel,
        out_shape=(
            jax.ShapeDtypeStruct((inlets // 2, 2 * LANES, 2 * plates), jnp.bfloat16),
            jax.ShapeDtypeStruct((inlets // 2, LANES, 2 * plates), f32),
            jax.ShapeDtypeStruct((8, LANES), f32),
        ),
        in_specs=[VMEM],
        out_specs=(VMEM,) * 3,
        compiler_params=pltpu.CompilerParams(vmem_limit_bytes=8 * 1024 * 1024),
        cost_estimate=pl.CostEstimate(flops=20000000, bytes_accessed=6400000, transcendentals=0),
        name="prepare",
    )(packed)

    wide = (3 * cz, cy + 2 * HALO, nx)
    tall = (wide[0], wide[1] + 2 * HALO, nx)
    cells = cz * cy
    copies = lax.axis_size("x")
    lines = tiles // (WIDTH * PACKED)
    payload, basis = pl.pallas_call(
        basis_kernel,
        out_shape=(
            jax.ShapeDtypeStruct((copies * WIDTH * (lines + 1), LANES), f32),
            jax.ShapeDtypeStruct(((DEGREE + 1) * cells, nx), f32),
        ),
        in_specs=[VMEM] * 5,
        out_specs=(VMEM, VMEM),
        scratch_shapes=[
            pltpu.VMEM(wide, f32),
            pltpu.VMEM(wide, f32),
            pltpu.VMEM(tall, f32),
            pltpu.VMEM(tall, f32),
            pltpu.VMEM((24 * 8, nx), f32),
            pltpu.VMEM((FIELDS * cells, 2 * nx), jnp.bfloat16),
            pltpu.VMEM((plates, LANES), f32),
        ],
        compiler_params=pltpu.CompilerParams(vmem_limit_bytes=8 * 1024 * 1024),
        name="basis",
    )(own, low, high, lanes_hot, rows_hot)

    group = copies * WIDTH
    arrived = lax.all_to_all(
        payload.reshape(group * (lines + 1), 1, LANES), ("x", "y"), 0, 0, tiled=True
    )
    ends = lax.axis_size("core") * lax.axis_size("z")
    rows = pl.pallas_call(
        functools.partial(rows_kernel, lines=lines),
        out_shape=jax.ShapeDtypeStruct((ends, LANES), f32),
        in_specs=[VMEM],
        out_specs=VMEM,
        compiler_params=pltpu.CompilerParams(vmem_limit_bytes=2 * 1024 * 1024),
        name="rows",
    )(arrived.reshape(group * (lines + 1), LANES))
    arrived = lax.all_to_all(rows.reshape(ends, 1, LANES), ("core", "z"), 0, 0, tiled=True)
    scale = float(1.0 / (devices * inlets) ** 0.5)
    solution, residual, flow = pl.pallas_call(
        functools.partial(final_kernel, scale=scale),
        out_shape=(
            jax.ShapeDtypeStruct((cells, nx), f32),
            jax.ShapeDtypeStruct((cells, nx), f32),
            jax.ShapeDtypeStruct((OWNED,), f32),
        ),
        in_specs=[VMEM, VMEM, VMEM],
        out_specs=(VMEM, VMEM, SMEM),
        compiler_params=pltpu.CompilerParams(vmem_limit_bytes=4 * 1024 * 1024),
        name="final",
    )(arrived.reshape(ends, LANES), basis, owner)
    return (solution.reshape(cz, cy, nx), residual.reshape(cz, cy, nx), flow)


def solution(mesh):
    slabs, tiles = mesh.devices.shape
    chips = mesh.devices.reshape(slabs // 2, 2, tiles // WIDTH, WIDTH)
    fine = jax.sharding.Mesh(chips, SLAB + TILE)
    in_specs = (
        P(SLAB, TILE, None),
        P(SLAB, TILE, None),
        P(SLAB, TILE, None, None),
        P(),
        P(TILE),
        P(TILE),
    )
    out_specs = (P(SLAB, TILE, None), P(SLAB, TILE, None), P(TILE))
    return jax.shard_map(
        on_device, mesh=fine, in_specs=in_specs, out_specs=out_specs, check_vma=False
    )
```

```python
import functools

import jax
import jax.numpy as jnp
from jax import lax
from jax.experimental import pallas as pl
from jax.experimental.pallas import tpu as pltpu
from jax.sharding import PartitionSpec as P

HALO = 8
DEGREE = 8
FIELDS = 8
OWNED = 4
WIDTH = 8
PACKED = 4
LANES = 128
HIGH_LANE = 48
LOW_LANE = 96
CENTER = 64
SLAB = ("x", "core")
TILE = ("z", "y")


def two_sum(a, b):
    s = a + b
    v = s - a
    return s, (a - (s - v)) + (b - v)


def quick_two_sum(a, b):
    s = a + b
    return s, b - (s - a)


def split(a):
    c = a * 4097.0
    high = c - (c - a)
    return high, a - high


def two_prod(a, b):
    p = a * b
    ah, al = split(a)
    bh, bl = split(b)
    return p, ((ah * bh - p) + ah * bl + al * bh) + al * bl


def dd_add(x, y):
    s, e = two_sum(x[0], y[0])
    return quick_two_sum(s, e + (x[1] + y[1]))


def dd_mul(x, y):
    p, e = two_prod(x[0], y[0])
    return quick_two_sum(p, e + (x[0] * y[1] + x[1] * y[0]))


def dd_scale(x, power):
    return x[0] * power, x[1] * power


def dd_neg(x):
    return -x[0], -x[1]


def dd_sum(terms):
    terms = list(terms)
    while len(terms) > 1:
        terms = [dd_add(*terms[at : at + 2]) if at + 1 < len(terms) else terms[at] for at in range(0, len(terms), 2)]
    return terms[0]


def lane_of(shape):
    return lax.broadcasted_iota(jnp.int32, shape, len(shape) - 1)


def one_hot(found, dtype):
    return jnp.where(found, 1.0, 0.0).astype(dtype)


def prepare_kernel(packed, lanes_hot, rows_hot, owner):
    steps, _, columns = rows_hot.shape
    inlets, plates = 2 * steps, columns // 2
    index = packed[:inlets].astype(jnp.int32)
    order = packed[inlets : inlets + 1].astype(jnp.int32)
    low = (index & 127).astype(jnp.float32)
    high = (index >> 7).astype(jnp.float32)
    both = jnp.concatenate([low, high], axis=0).astype(jnp.bfloat16)
    row = lax.broadcasted_iota(jnp.int32, (plates, plates), 0)
    column = lane_of((plates, plates))
    group = column // (PACKED * OWNED)
    line, y = group // WIDTH, group % WIDTH
    place, q = (column // OWNED) % PACKED, column % OWNED
    owned = ((line * PACKED + place) * WIDTH + y) * OWNED + q
    for choice in (row == order, row == owned):
        both = jnp.dot(both, one_hot(choice, jnp.bfloat16), preferred_element_type=jnp.float32)
        both = both.astype(jnp.bfloat16)
    cells = both.astype(jnp.float32).astype(jnp.int32)
    at = lax.broadcasted_iota(jnp.int32, (LANES, plates), 0)
    for slot in range(inlets):
        step, start = slot // 2, (slot % 2) * plates
        hot = one_hot(at == cells[slot : slot + 1], jnp.bfloat16)
        lanes_hot[step, :LANES, start : start + plates] = hot
        lanes_hot[step, LANES:, start : start + plates] = hot
        rows_hot[step, :, start : start + plates] = one_hot(
            at == cells[inlets + slot : inlets + slot + 1], jnp.float32
        )
    lane = lane_of((8, LANES))
    first = lax.broadcasted_iota(jnp.int32, (8, LANES), 0) == 0
    values = jnp.zeros((8, LANES), jnp.float32)
    for q in range(OWNED):
        own, other = (packed[inlets + 1 : inlets + 2, at : at + 1] for at in (q, OWNED + q))
        values = jnp.where(lane == q * FIELDS, jnp.where(first, own, other), values)
    owner[...] = values


def basis_kernel(
    own, low, high, lanes_hot, rows_hot, payload, basis,
    alpha, beta, even, odd, parts, halves, turned,
):
    cz = own.shape[1]
    wide_y = own.shape[2]
    cy = wide_y - 2 * HALO
    for place, source in enumerate((low, own, high)):
        at = pl.ds(place * cz, cz)
        even[at, HALO : HALO + wide_y, :] = source[0]
        diag = source[1]
        inside = jnp.where(diag > 0.0, 0.25, 0.0)
        beta[at] = inside
        alpha[at] = (diag - 1.0) * inside
    lane = lane_of((wide_y, LANES))
    planes = 3 * cz
    edge = jnp.zeros((planes, HALO, LANES), jnp.float32)
    for field in (even, odd):
        field[:, :HALO, :] = edge
        field[:, HALO + wide_y :, :] = edge
    rows = pl.ds(HALO, wide_y)
    inner = pl.ds(2 * HALO, cy)

    cells = cz * cy

    def emit(field, degree):
        for z in range(cz):
            value = field[cz + z, inner, :]
            at = pl.ds(degree * cells + z * cy, cy)
            basis[at, :] = value
            if degree < FIELDS:
                upper = value.astype(jnp.bfloat16)
                halves[at, :LANES] = upper
                halves[at, LANES:] = (value - upper.astype(jnp.float32)).astype(jnp.bfloat16)

    def product(first, second, slot):
        total = None
        for z in range(cz):
            term = first[cz + z, inner, :] * second[cz + z, inner, :]
            term = term[:8] + term[8:]
            total = term if total is None else total + term
        parts[pl.ds(slot * 8, 8), :] = total

    emit(even, 0)
    product(even, even, 0)
    now, later = even, odd
    for degree in range(DEGREE):

        def plane(z, now=now, later=later, degree=degree):
            value = now[z, rows, :]
            beside = now[z - 1, rows, :] + now[z + 1, rows, :]
            beside = beside + now[z, pl.ds(HALO - 1, wide_y), :] + now[z, pl.ds(HALO + 1, wide_y), :]
            beside = beside + jnp.where(lane == 0, 0.0, pltpu.roll(value, 1, 1))
            beside = beside + jnp.where(lane == LANES - 1, 0.0, pltpu.roll(value, LANES - 1, 1))
            fresh = alpha[z] * value - beta[z] * beside
            if degree == 0:
                later[z, rows, :] = 0.5 * fresh
            else:
                later[z, rows, :] = fresh - later[z, rows, :]

        for z in range(degree + 1, planes - 1 - degree):
            plane(z)
        emit(later, degree + 1)
        product(now, later, 2 * degree + 1)
        product(later, later, 2 * degree + 2)
        now, later = later, now

    slots = parts.shape[0] // 8
    for slot in range(2 * DEGREE + 1, slots):
        parts[pl.ds(slot * 8, 8), :] = jnp.zeros((8, LANES), jnp.float32)
    value = parts[pl.ds(0, slots, stride=8), :]
    error = jnp.zeros_like(value)
    for row in range(1, 8):
        value, extra = two_sum(value, parts[pl.ds(row, slots, stride=8), :])
        error = error + extra
    step = LANES // 2
    while step:
        value, extra = two_sum(value, pltpu.roll(value, step, 1))
        error = error + pltpu.roll(error, step, 1) + extra
        step //= 2
    lane_s = lane_of((slots, LANES))
    row_s = lax.broadcasted_iota(jnp.int32, (slots, LANES), 0)
    parity = row_s % 2 == 0
    base = jnp.where(parity, value[0:1], value[1:2])
    base_error = jnp.where(parity, error[0:1], error[1:2])
    value, extra = two_sum(2.0 * value, -base)
    error = (2.0 * error - base_error) + extra
    value, error = quick_two_sum(value, error)
    placed = jnp.where(jnp.abs(lane_s - HIGH_LANE) == row_s, value, 0.0)
    placed = placed + jnp.where(jnp.abs(lane_s - LOW_LANE) == row_s, error, 0.0)
    placed = jnp.where(row_s <= 2 * DEGREE, placed, 0.0)
    moments = jnp.sum(placed, axis=0, keepdims=True)

    steps, depth, columns = rows_hot.shape
    plates = columns // 2
    tile = 2 * LANES
    groups = plates // LANES

    totals = [jnp.zeros((FIELDS, 8, LANES), jnp.float32)] * groups
    for step in range(steps):
        for start in range(0, columns, tile):
            picked = jnp.dot(
                halves[...], lanes_hot[step, :, start : start + tile], preferred_element_type=jnp.float32
            )
            mask = rows_hot[step, :, start : start + tile].reshape(1, depth // 8, 8, tile)
            picked = jnp.sum(picked.reshape(FIELDS, depth // 8, 8, tile) * mask, axis=1)
            for side in range(2):
                group = (start // LANES + side) % groups
                totals[group] = totals[group] + picked[:, :, side * LANES : (side + 1) * LANES]
    for group, total in enumerate(totals):
        turned[pl.ds(group * LANES, LANES), :FIELDS] = jnp.sum(total, axis=1).T

    lines = plates // (OWNED * WIDTH * PACKED)
    rows_per = WIDTH * (lines + 1)
    sources = payload.shape[0] // rows_per
    packed = PACKED * OWNED
    lane_w = lane_of((lines * WIDTH, LANES))
    out = jnp.zeros((lines * WIDTH, LANES), jnp.float32)
    for at in range(packed):
        column = turned[pl.ds(at, lines * WIDTH, stride=packed), :]
        if at:
            column = pltpu.roll(column, at * FIELDS, 1)
        out = jnp.where(lane_w // FIELDS == at, column, out)
    for line in range(lines):
        for at in range(sources):
            payload[pl.ds(at * rows_per + line, WIDTH, stride=lines + 1), :] = out[line * WIDTH : (line + 1) * WIDTH]
    out = jnp.broadcast_to(moments, (WIDTH, LANES))
    for at in range(sources):
        payload[pl.ds(at * rows_per + lines, WIDTH, stride=lines + 1), :] = out


def with_error(value, error):
    lane = lane_of(value.shape)
    shifted = pltpu.roll(error, LOW_LANE - HIGH_LANE, 1)
    first = lane < OWNED * FIELDS
    return value + jnp.where(first, error, 0.0) + jnp.where(lane >= LOW_LANE - 2 * DEGREE, shifted, 0.0)


def sum_rows(rows, step):
    value = rows[pl.ds(0, 8), :]
    error = jnp.zeros_like(value)
    for at in range(8, rows.shape[0], 8):
        value, extra = two_sum(value, rows[pl.ds(at, 8), :])
        error = error + extra
    while step < 8:
        value, extra = two_sum(value, pltpu.roll(value, step, 0))
        error = error + pltpu.roll(error, step, 0) + extra
        step *= 2
    return value, error


def rows_kernel(rows, out, lines=1):
    value, error = sum_rows(rows, lines + 1)
    moments = with_error(value, error)[lines : lines + 1]
    total = value + error
    depth = lines * PACKED
    row = lax.broadcasted_iota(jnp.int32, (8, LANES), 0)
    first = lane_of((1, LANES)) < OWNED * FIELDS
    made = []
    for z in range(depth):
        line = total[z // PACKED : z // PACKED + 1]
        place = (z % PACKED) * OWNED * FIELDS
        if place:
            line = pltpu.roll(line, LANES - place, 1)
        made.append(jnp.where(first, line, moments))
    for at in range(0, out.shape[0], depth):
        for z in range(depth):
            out[pl.ds(at + z, 1), :] = made[z]


def shift(row, amount):
    return pltpu.roll(row, (-amount) % LANES, 1)


def apply_operator(coeffs):
    count = len(coeffs)
    terms = [[] for _ in range(count + 1)]
    for j, value in enumerate(coeffs):
        terms[j].append(dd_add(dd_scale(value, 8.0), dd_neg(value)))
        if j == 0:
            terms[1].append(dd_scale(value, 8.0))
        else:
            terms[j + 1].append(dd_scale(value, 4.0))
            terms[j - 1].append(dd_scale(value, 4.0))
    return [dd_sum(group) for group in terms]


def multiply(left, right):
    terms = [[] for _ in range(len(left) + len(right) - 1)]
    for i, a in enumerate(left):
        for j, b in enumerate(right):
            half = dd_scale(dd_mul(a, b), 0.5)
            terms[i + j].append(half)
            terms[abs(i - j)].append(half)
    return [dd_sum(group) for group in terms]


def square(values):
    terms = [[] for _ in range(2 * len(values) - 1)]
    for i, a in enumerate(values):
        for j in range(i, len(values)):
            term = dd_mul(a, values[j])
            if i == j:
                term = dd_scale(term, 0.5)
            terms[i + j].append(term)
            terms[j - i].append(term)
    return [dd_sum(group) for group in terms]


def galerkin(folded):
    high, low = folded
    moment = high + low
    beside = dd_add((shift(high, 1), shift(low, 1)), (shift(high, -1), shift(low, -1)))
    eight = dd_scale(folded, 8.0)
    weight = dd_add(dd_add(dd_scale(beside, 4.0), eight), dd_neg(folded))
    weight = weight[0] + weight[1]

    def entry(source, j):
        return jnp.broadcast_to(source[:, CENTER + j : CENTER + j + 1], source.shape)

    weights = [entry(weight, j) for j in range(7)]
    rhs = [entry(moment, j) for j in range(4)]
    matrix = [[0.5 * (weights[i + j] + weights[abs(i - j)]) for j in range(4)] for i in range(4)]
    inverse = []
    for k in range(4):
        inverse.append(1.0 / matrix[k][k])
        for i in range(k + 1, 4):
            factor = matrix[i][k] * inverse[k]
            for j in range(k + 1, i + 1):
                matrix[i][j] = matrix[i][j] - factor * matrix[j][k]
            rhs[i] = rhs[i] - factor * rhs[k]
    result = [None] * 4
    for i in range(3, -1, -1):
        value = rhs[i]
        for j in range(i + 1, 4):
            value = value - matrix[j][i] * result[j]
        result[i] = value * inverse[i]
    return result


def final_kernel(rows, basis, owner, solution, residual, flow, scale=1.0):
    row = with_error(*sum_rows(rows, 1))
    lane = lane_of((8, LANES))
    valid = jnp.abs(lane - CENTER) <= 2 * DEGREE
    high = jnp.where(valid, pltpu.roll(row, CENTER - HIGH_LANE, 1), 0.0)
    low = jnp.where(valid, pltpu.roll(row, LANES + CENTER - LOW_LANE, 1), 0.0)
    mu = quick_two_sum(high, low)
    zero = jnp.zeros((8, LANES), jnp.float32)
    first_coeffs = galerkin(mu)
    change = apply_operator([(value, zero) for value in first_coeffs])
    poly = [dd_neg(value) for value in change]
    poly[0] = dd_add(poly[0], (zero + 1.0, zero))
    terms = []
    for c, value in enumerate(square(poly)):
        if c == 0:
            overlap = mu
        else:
            up = (shift(mu[0], c), shift(mu[1], c))
            down = (shift(mu[0], -c), shift(mu[1], -c))
            overlap = dd_scale(dd_add(up, down), 0.5)
        terms.append(dd_mul(value, overlap))
    nu = dd_sum(terms)
    second_coeffs = galerkin(nu)
    gain = multiply([(value, zero) for value in second_coeffs], poly)
    drop = apply_operator(gain)
    solved = list(gain)
    for j in range(4):
        solved[j] = dd_add(gain[j], (first_coeffs[j], zero))
    left = [dd_neg(value) for value in drop]
    for j in range(5):
        left[j] = dd_add(left[j], poly[j])
    solved = [value[0] + value[1] for value in solved]
    left = [value[0] + value[1] for value in left]

    cells = solution.shape[0]
    for at in range(0, cells, 8):
        fields = [basis[pl.ds(k * cells + at, 8), :] for k in range(DEGREE + 1)]
        total = solved[0] * fields[0]
        rest = left[0] * fields[0]
        for k in range(1, DEGREE + 1):
            if k < FIELDS:
                total = total + solved[k] * fields[k]
            rest = rest + left[k] * fields[k]
        solution[pl.ds(at, 8), :] = total
        residual[pl.ds(at, 8), :] = rest

    weights = zero
    for k in range(FIELDS):
        weights = jnp.where(lane % FIELDS == k, solved[k], weights)
    header = row * weights
    for step in (4, 2, 1):
        header = header + shift(header, step)
    result = owner[0:1, :] * (header[0:1, :] * scale - owner[1:2, :])
    for q in range(OWNED):
        flow[q] = result[0, q * FIELDS]


VMEM = pl.BlockSpec(memory_space=pltpu.VMEM)
SMEM = pl.BlockSpec(memory_space=pltpu.SMEM)


def on_device(right_side, diagonal, inlet_index, plate_order, conductance, plate_level):
    cz, cy, nx = right_side.shape
    tiles = lax.axis_size(TILE)
    devices = lax.axis_size(SLAB) * tiles
    plates, inlets = inlet_index.shape[2:]
    f32 = jnp.float32

    def swap(value, axis, start):
        pairs = [(i, i + 1) for i in range(start, lax.axis_size(axis) - 1, 2)]
        return lax.ppermute(value, axis, pairs + [(target, source) for source, target in pairs])

    own = lax.optimization_barrier(jnp.stack([right_side, diagonal]))
    even = lax.axis_index(TILE) % 2 == 0
    first, last = own[:, :, :HALO], own[:, :, cy - HALO :]
    outer = swap(jnp.where(even, first, last), TILE, 1)
    inner = swap(jnp.where(even, last, first), TILE, 0)
    before, after = jnp.where(even, outer, inner), jnp.where(even, inner, outer)
    own = jnp.concatenate([before, own, after], axis=2)
    owned = jnp.pad(jnp.concatenate([conductance, plate_level]), (0, plates - 2 * OWNED))
    packed = jnp.concatenate([inlet_index[0, 0].T.astype(f32), plate_order.astype(f32)[None], owned[None]])
    odd = lax.axis_index(SLAB) % 2 == 1
    near = jnp.where(odd, own[:, ::-1], own)
    middle = slice(HALO, HALO + cy)
    sides = jnp.concatenate([near[:, :, :HALO], near[:, :, HALO + cy :]], axis=2)
    sent = [near[0, :, middle], near[1, : cz - 1, middle], sides[0, : cz - 1], sides[1, : cz - 2]]
    arrived = swap(jnp.concatenate(sent), SLAB, 1)
    inner = swap(own, SLAB, 0)
    pieces, start = [], 0
    for piece in sent:
        count = piece.shape[0]
        pieces.append(jnp.pad(arrived[start : start + count], ((0, cz - count), (0, 0), (0, 0))))
        start += count
    middle, sides = jnp.stack(pieces[:2]), jnp.stack(pieces[2:])
    outer = jnp.concatenate([sides[:, :, :HALO], middle, sides[:, :, HALO:]], axis=2)
    low, high = jnp.where(odd, inner, outer[:, ::-1]), jnp.where(odd, outer, inner)

    lanes_hot, rows_hot, owner = pl.pallas_call(
        prepare_kernel,
        out_shape=(
            jax.ShapeDtypeStruct((inlets // 2, 2 * LANES, 2 * plates), jnp.bfloat16),
            jax.ShapeDtypeStruct((inlets // 2, LANES, 2 * plates), f32),
            jax.ShapeDtypeStruct((8, LANES), f32),
        ),
        in_specs=[VMEM],
        out_specs=(VMEM,) * 3,
        compiler_params=pltpu.CompilerParams(vmem_limit_bytes=8 * 1024 * 1024),
        cost_estimate=pl.CostEstimate(flops=20000000, bytes_accessed=6400000, transcendentals=0),
        name="prepare",
    )(packed)

    wide = (3 * cz, cy + 2 * HALO, nx)
    tall = (wide[0], wide[1] + 2 * HALO, nx)
    cells = cz * cy
    copies = lax.axis_size("x")
    lines = tiles // (WIDTH * PACKED)
    payload, basis = pl.pallas_call(
        basis_kernel,
        out_shape=(
            jax.ShapeDtypeStruct((copies * WIDTH * (lines + 1), LANES), f32),
            jax.ShapeDtypeStruct(((DEGREE + 1) * cells, nx), f32),
        ),
        in_specs=[VMEM] * 5,
        out_specs=(VMEM, VMEM),
        scratch_shapes=[
            pltpu.VMEM(wide, f32),
            pltpu.VMEM(wide, f32),
            pltpu.VMEM(tall, f32),
            pltpu.VMEM(tall, f32),
            pltpu.VMEM((24 * 8, nx), f32),
            pltpu.VMEM((FIELDS * cells, 2 * nx), jnp.bfloat16),
            pltpu.VMEM((plates, LANES), f32),
        ],
        compiler_params=pltpu.CompilerParams(vmem_limit_bytes=8 * 1024 * 1024),
        name="basis",
    )(own, low, high, lanes_hot, rows_hot)

    group = copies * WIDTH
    arrived = lax.all_to_all(
        payload.reshape(group * (lines + 1), 1, LANES), ("x", "y"), 0, 0, tiled=True
    )
    ends = lax.axis_size("core") * lax.axis_size("z")
    rows = pl.pallas_call(
        functools.partial(rows_kernel, lines=lines),
        out_shape=jax.ShapeDtypeStruct((ends, LANES), f32),
        in_specs=[VMEM],
        out_specs=VMEM,
        compiler_params=pltpu.CompilerParams(vmem_limit_bytes=2 * 1024 * 1024),
        name="rows",
    )(arrived.reshape(group * (lines + 1), LANES))
    arrived = lax.all_to_all(rows.reshape(ends, 1, LANES), ("core", "z"), 0, 0, tiled=True)
    scale = float(1.0 / (devices * inlets) ** 0.5)
    solution, residual, flow = pl.pallas_call(
        functools.partial(final_kernel, scale=scale),
        out_shape=(
            jax.ShapeDtypeStruct((cells, nx), f32),
            jax.ShapeDtypeStruct((cells, nx), f32),
            jax.ShapeDtypeStruct((OWNED,), f32),
        ),
        in_specs=[VMEM, VMEM, VMEM],
        out_specs=(VMEM, VMEM, SMEM),
        compiler_params=pltpu.CompilerParams(vmem_limit_bytes=4 * 1024 * 1024),
        name="final",
    )(arrived.reshape(ends, LANES), basis, owner)
    return (solution.reshape(cz, cy, nx), residual.reshape(cz, cy, nx), flow)


def solution(mesh):
    slabs, tiles = mesh.devices.shape
    chips = mesh.devices.reshape(slabs // 2, 2, tiles // WIDTH, WIDTH)
    fine = jax.sharding.Mesh(chips, SLAB + TILE)
    in_specs = (
        P(SLAB, TILE, None),
        P(SLAB, TILE, None),
        P(SLAB, TILE, None, None),
        P(),
        P(TILE),
        P(TILE),
    )
    out_specs = (P(SLAB, TILE, None), P(SLAB, TILE, None), P(TILE))
    return jax.shard_map(
        on_device, mesh=fine, in_specs=in_specs, out_specs=out_specs, check_vma=False
    )
```

```python
import functools

import jax
import jax.numpy as jnp
from jax import lax
from jax.experimental import pallas as pl
from jax.experimental.pallas import tpu as pltpu
from jax.sharding import PartitionSpec as P

HALO = 8
DEGREE = 8
FIELDS = 8
OWNED = 4
WIDTH = 8
PACKED = 4
LANES = 128
HIGH_LANE = 48
LOW_LANE = 96
CENTER = 64
SLAB = ("x", "core")
TILE = ("z", "y")


def two_sum(a, b):
    s = a + b
    v = s - a
    return s, (a - (s - v)) + (b - v)


def quick_two_sum(a, b):
    s = a + b
    return s, b - (s - a)


def split(a):
    c = a * 4097.0
    high = c - (c - a)
    return high, a - high


def two_prod(a, b):
    p = a * b
    ah, al = split(a)
    bh, bl = split(b)
    return p, ((ah * bh - p) + ah * bl + al * bh) + al * bl


def dd_add(x, y):
    s, e = two_sum(x[0], y[0])
    return quick_two_sum(s, e + (x[1] + y[1]))


def dd_mul(x, y):
    p, e = two_prod(x[0], y[0])
    return quick_two_sum(p, e + (x[0] * y[1] + x[1] * y[0]))


def dd_scale(x, power):
    return x[0] * power, x[1] * power


def dd_neg(x):
    return -x[0], -x[1]


def dd_sum(terms):
    terms = list(terms)
    while len(terms) > 1:
        terms = [dd_add(*terms[at : at + 2]) if at + 1 < len(terms) else terms[at] for at in range(0, len(terms), 2)]
    return terms[0]


def lane_of(shape):
    return lax.broadcasted_iota(jnp.int32, shape, len(shape) - 1)


def one_hot(found, dtype):
    return jnp.where(found, 1.0, 0.0).astype(dtype)


def prepare_kernel(packed, lanes_hot, rows_hot, owner):
    steps, _, columns = rows_hot.shape
    inlets, plates = 2 * steps, columns // 2
    index = packed[:inlets].astype(jnp.int32)
    order = packed[inlets : inlets + 1].astype(jnp.int32)
    low = (index & 127).astype(jnp.float32)
    high = (index >> 7).astype(jnp.float32)
    both = jnp.concatenate([low, high], axis=0).astype(jnp.bfloat16)
    row = lax.broadcasted_iota(jnp.int32, (plates, plates), 0)
    column = lane_of((plates, plates))
    group = column // (PACKED * OWNED)
    line, y = group // WIDTH, group % WIDTH
    place, q = (column // OWNED) % PACKED, column % OWNED
    owned = ((line * PACKED + place) * WIDTH + y) * OWNED + q
    for choice in (row == order, row == owned):
        both = jnp.dot(both, one_hot(choice, jnp.bfloat16), preferred_element_type=jnp.float32)
        both = both.astype(jnp.bfloat16)
    cells = both.astype(jnp.float32).astype(jnp.int32)
    at = lax.broadcasted_iota(jnp.int32, (LANES, plates), 0)
    for slot in range(inlets):
        step, start = slot // 2, (slot % 2) * plates
        hot = one_hot(at == cells[slot : slot + 1], jnp.bfloat16)
        lanes_hot[step, :LANES, start : start + plates] = hot
        lanes_hot[step, LANES:, start : start + plates] = hot
        rows_hot[step, :, start : start + plates] = one_hot(
            at == cells[inlets + slot : inlets + slot + 1], jnp.float32
        )
    lane = lane_of((8, LANES))
    first = lax.broadcasted_iota(jnp.int32, (8, LANES), 0) == 0
    values = jnp.zeros((8, LANES), jnp.float32)
    for q in range(OWNED):
        own, other = (packed[inlets + 1 : inlets + 2, at : at + 1] for at in (q, OWNED + q))
        values = jnp.where(lane == q * FIELDS, jnp.where(first, own, other), values)
    owner[...] = values


def basis_kernel(
    own, low, high, lanes_hot, rows_hot, payload, basis,
    alpha, beta, even, odd, parts, halves, turned,
):
    cz = own.shape[1]
    wide_y = own.shape[2]
    cy = wide_y - 2 * HALO
    for place, source in enumerate((low, own, high)):
        at = pl.ds(place * cz, cz)
        even[at, HALO : HALO + wide_y, :] = source[0]
        diag = source[1]
        inside = jnp.where(diag > 0.0, 0.25, 0.0)
        beta[at] = inside
        alpha[at] = (diag - 1.0) * inside
    lane = lane_of((wide_y, LANES))
    planes = 3 * cz
    edge = jnp.zeros((planes, HALO, LANES), jnp.float32)
    for field in (even, odd):
        field[:, :HALO, :] = edge
        field[:, HALO + wide_y :, :] = edge
    rows = pl.ds(HALO, wide_y)
    inner = pl.ds(2 * HALO, cy)

    cells = cz * cy

    def emit(field, degree):
        for z in range(cz):
            value = field[cz + z, inner, :]
            at = pl.ds(degree * cells + z * cy, cy)
            basis[at, :] = value
            if degree < FIELDS:
                upper = value.astype(jnp.bfloat16)
                halves[at, :LANES] = upper
                halves[at, LANES:] = (value - upper.astype(jnp.float32)).astype(jnp.bfloat16)

    def product(first, second, slot):
        total = None
        for z in range(cz):
            term = first[cz + z, inner, :] * second[cz + z, inner, :]
            term = term[:8] + term[8:]
            total = term if total is None else total + term
        parts[pl.ds(slot * 8, 8), :] = total

    emit(even, 0)
    product(even, even, 0)
    now, later = even, odd
    for degree in range(DEGREE):

        def plane(z, now=now, later=later, degree=degree):
            value = now[z, rows, :]
            beside = now[z - 1, rows, :] + now[z + 1, rows, :]
            beside = beside + now[z, pl.ds(HALO - 1, wide_y), :] + now[z, pl.ds(HALO + 1, wide_y), :]
            beside = beside + jnp.where(lane == 0, 0.0, pltpu.roll(value, 1, 1))
            beside = beside + jnp.where(lane == LANES - 1, 0.0, pltpu.roll(value, LANES - 1, 1))
            fresh = alpha[z] * value - beta[z] * beside
            if degree == 0:
                later[z, rows, :] = 0.5 * fresh
            else:
                later[z, rows, :] = fresh - later[z, rows, :]

        for z in range(degree + 1, planes - 1 - degree):
            plane(z)
        emit(later, degree + 1)
        product(now, later, 2 * degree + 1)
        product(later, later, 2 * degree + 2)
        now, later = later, now

    slots = parts.shape[0] // 8
    for slot in range(2 * DEGREE + 1, slots):
        parts[pl.ds(slot * 8, 8), :] = jnp.zeros((8, LANES), jnp.float32)
    value = parts[pl.ds(0, slots, stride=8), :]
    error = jnp.zeros_like(value)
    for row in range(1, 8):
        value, extra = two_sum(value, parts[pl.ds(row, slots, stride=8), :])
        error = error + extra
    step = LANES // 2
    while step:
        value, extra = two_sum(value, pltpu.roll(value, step, 1))
        error = error + pltpu.roll(error, step, 1) + extra
        step //= 2
    lane_s = lane_of((slots, LANES))
    row_s = lax.broadcasted_iota(jnp.int32, (slots, LANES), 0)
    parity = row_s % 2 == 0
    base = jnp.where(parity, value[0:1], value[1:2])
    base_error = jnp.where(parity, error[0:1], error[1:2])
    value, extra = two_sum(2.0 * value, -base)
    error = (2.0 * error - base_error) + extra
    value, error = quick_two_sum(value, error)
    placed = jnp.where(jnp.abs(lane_s - HIGH_LANE) == row_s, value, 0.0)
    placed = placed + jnp.where(jnp.abs(lane_s - LOW_LANE) == row_s, error, 0.0)
    placed = jnp.where(row_s <= 2 * DEGREE, placed, 0.0)
    moments = jnp.sum(placed, axis=0, keepdims=True)

    steps, depth, columns = rows_hot.shape
    plates = columns // 2
    tile = 2 * LANES
    groups = plates // LANES

    totals = [jnp.zeros((FIELDS, 8, LANES), jnp.float32)] * groups
    for step in range(steps):
        for start in range(0, columns, tile):
            picked = jnp.dot(
                halves[...], lanes_hot[step, :, start : start + tile], preferred_element_type=jnp.float32
            )
            mask = rows_hot[step, :, start : start + tile].reshape(1, depth // 8, 8, tile)
            picked = jnp.sum(picked.reshape(FIELDS, depth // 8, 8, tile) * mask, axis=1)
            for side in range(2):
                group = (start // LANES + side) % groups
                totals[group] = totals[group] + picked[:, :, side * LANES : (side + 1) * LANES]
    for group, total in enumerate(totals):
        turned[pl.ds(group * LANES, LANES), :FIELDS] = jnp.sum(total, axis=1).T

    lines = plates // (OWNED * WIDTH * PACKED)
    rows_per = WIDTH * (lines + 1)
    sources = payload.shape[0] // rows_per
    packed = PACKED * OWNED
    lane_w = lane_of((lines * WIDTH, LANES))
    out = jnp.zeros((lines * WIDTH, LANES), jnp.float32)
    for at in range(packed):
        column = turned[pl.ds(at, lines * WIDTH, stride=packed), :]
        if at:
            column = pltpu.roll(column, at * FIELDS, 1)
        out = jnp.where(lane_w // FIELDS == at, column, out)
    for line in range(lines):
        for at in range(sources):
            payload[pl.ds(at * rows_per + line, WIDTH, stride=lines + 1), :] = out[line * WIDTH : (line + 1) * WIDTH]
    out = jnp.broadcast_to(moments, (WIDTH, LANES))
    for at in range(sources):
        payload[pl.ds(at * rows_per + lines, WIDTH, stride=lines + 1), :] = out


def with_error(value, error):
    lane = lane_of(value.shape)
    shifted = pltpu.roll(error, LOW_LANE - HIGH_LANE, 1)
    first = lane < OWNED * FIELDS
    return value + jnp.where(first, error, 0.0) + jnp.where(lane >= LOW_LANE - 2 * DEGREE, shifted, 0.0)


def sum_rows(rows, step):
    value = rows[pl.ds(0, 8), :]
    error = jnp.zeros_like(value)
    for at in range(8, rows.shape[0], 8):
        value, extra = two_sum(value, rows[pl.ds(at, 8), :])
        error = error + extra
    while step < 8:
        value, extra = two_sum(value, pltpu.roll(value, step, 0))
        error = error + pltpu.roll(error, step, 0) + extra
        step *= 2
    return value, error


def rows_kernel(rows, out, lines=1):
    value, error = sum_rows(rows, lines + 1)
    moments = with_error(value, error)[lines : lines + 1]
    total = value + error
    depth = lines * PACKED
    row = lax.broadcasted_iota(jnp.int32, (8, LANES), 0)
    first = lane_of((1, LANES)) < OWNED * FIELDS
    made = []
    for z in range(depth):
        line = total[z // PACKED : z // PACKED + 1]
        place = (z % PACKED) * OWNED * FIELDS
        if place:
            line = pltpu.roll(line, LANES - place, 1)
        made.append(jnp.where(first, line, moments))
    for at in range(0, out.shape[0], depth):
        for z in range(depth):
            out[pl.ds(at + z, 1), :] = made[z]


def shift(row, amount):
    return pltpu.roll(row, (-amount) % LANES, 1)


def apply_operator(coeffs):
    count = len(coeffs)
    terms = [[] for _ in range(count + 1)]
    for j, value in enumerate(coeffs):
        terms[j].append(dd_add(dd_scale(value, 8.0), dd_neg(value)))
        if j == 0:
            terms[1].append(dd_scale(value, 8.0))
        else:
            terms[j + 1].append(dd_scale(value, 4.0))
            terms[j - 1].append(dd_scale(value, 4.0))
    return [dd_sum(group) for group in terms]


def multiply(left, right):
    terms = [[] for _ in range(len(left) + len(right) - 1)]
    for i, a in enumerate(left):
        for j, b in enumerate(right):
            product, error = two_prod(a, b[0])
            half = dd_scale(quick_two_sum(product, error + a * b[1]), 0.5)
            terms[i + j].append(half)
            terms[abs(i - j)].append(half)
    return [dd_sum(group) for group in terms]


def square(values):
    terms = [[] for _ in range(2 * len(values) - 1)]
    for i, a in enumerate(values):
        for j in range(i, len(values)):
            term = dd_mul(a, values[j])
            if i == j:
                term = dd_scale(term, 0.5)
            terms[i + j].append(term)
            terms[j - i].append(term)
    return [dd_sum(group) for group in terms]


def galerkin(folded):
    high, low = folded
    moment = high + low
    beside = dd_add((shift(high, 1), shift(low, 1)), (shift(high, -1), shift(low, -1)))
    eight = dd_scale(folded, 8.0)
    weight = dd_add(dd_add(dd_scale(beside, 4.0), eight), dd_neg(folded))
    weight = weight[0] + weight[1]

    def entry(source, j):
        return jnp.broadcast_to(source[:, CENTER + j : CENTER + j + 1], source.shape)

    weights = [entry(weight, j) for j in range(7)]
    rhs = [entry(moment, j) for j in range(4)]
    matrix = [[0.5 * (weights[i + j] + weights[abs(i - j)]) for j in range(4)] for i in range(4)]
    inverse = []
    for k in range(4):
        inverse.append(1.0 / matrix[k][k])
        for i in range(k + 1, 4):
            factor = matrix[i][k] * inverse[k]
            for j in range(k + 1, i + 1):
                matrix[i][j] = matrix[i][j] - factor * matrix[j][k]
            rhs[i] = rhs[i] - factor * rhs[k]
    result = [None] * 4
    for i in range(3, -1, -1):
        value = rhs[i]
        for j in range(i + 1, 4):
            value = value - matrix[j][i] * result[j]
        result[i] = value * inverse[i]
    return result


def final_kernel(rows, basis, owner, solution, residual, flow, scale=1.0):
    row = with_error(*sum_rows(rows, 1))
    lane = lane_of((8, LANES))
    valid = jnp.abs(lane - CENTER) <= 2 * DEGREE
    high = jnp.where(valid, pltpu.roll(row, CENTER - HIGH_LANE, 1), 0.0)
    low = jnp.where(valid, pltpu.roll(row, LANES + CENTER - LOW_LANE, 1), 0.0)
    mu = quick_two_sum(high, low)
    zero = jnp.zeros((8, LANES), jnp.float32)
    first_coeffs = galerkin(mu)
    change = apply_operator([(value, zero) for value in first_coeffs])
    poly = [dd_neg(value) for value in change]
    poly[0] = dd_add(poly[0], (zero + 1.0, zero))
    terms = []
    for c, value in enumerate(square(poly)):
        if c == 0:
            overlap = mu
        else:
            up = (shift(mu[0], c), shift(mu[1], c))
            down = (shift(mu[0], -c), shift(mu[1], -c))
            overlap = dd_scale(dd_add(up, down), 0.5)
        terms.append(dd_mul(value, overlap))
    nu = dd_sum(terms)
    second_coeffs = galerkin(nu)
    gain = multiply(second_coeffs, poly)
    drop = apply_operator(gain)
    solved = list(gain)
    for j in range(4):
        solved[j] = dd_add(gain[j], (first_coeffs[j], zero))
    left = [dd_neg(value) for value in drop]
    for j in range(5):
        left[j] = dd_add(left[j], poly[j])
    solved = [value[0] + value[1] for value in solved]
    left = [value[0] + value[1] for value in left]

    cells = solution.shape[0]
    for at in range(0, cells, 8):
        fields = [basis[pl.ds(k * cells + at, 8), :] for k in range(DEGREE + 1)]
        total = solved[0] * fields[0]
        rest = left[0] * fields[0]
        for k in range(1, DEGREE + 1):
            if k < FIELDS:
                total = total + solved[k] * fields[k]
            rest = rest + left[k] * fields[k]
        solution[pl.ds(at, 8), :] = total
        residual[pl.ds(at, 8), :] = rest

    weights = zero
    for k in range(FIELDS):
        weights = jnp.where(lane % FIELDS == k, solved[k], weights)
    header = row * weights
    for step in (4, 2, 1):
        header = header + shift(header, step)
    result = owner[0:1, :] * (header[0:1, :] * scale - owner[1:2, :])
    for q in range(OWNED):
        flow[q] = result[0, q * FIELDS]


VMEM = pl.BlockSpec(memory_space=pltpu.VMEM)
SMEM = pl.BlockSpec(memory_space=pltpu.SMEM)


def on_device(right_side, diagonal, inlet_index, plate_order, conductance, plate_level):
    cz, cy, nx = right_side.shape
    tiles = lax.axis_size(TILE)
    devices = lax.axis_size(SLAB) * tiles
    plates, inlets = inlet_index.shape[2:]
    f32 = jnp.float32

    def swap(value, axis, start):
        pairs = [(i, i + 1) for i in range(start, lax.axis_size(axis) - 1, 2)]
        return lax.ppermute(value, axis, pairs + [(target, source) for source, target in pairs])

    own = lax.optimization_barrier(jnp.stack([right_side, diagonal]))
    even = lax.axis_index(TILE) % 2 == 0
    first, last = own[:, :, :HALO], own[:, :, cy - HALO :]
    outer = swap(jnp.where(even, first, last), TILE, 1)
    inner = swap(jnp.where(even, last, first), TILE, 0)
    before, after = jnp.where(even, outer, inner), jnp.where(even, inner, outer)
    own = jnp.concatenate([before, own, after], axis=2)
    owned = jnp.pad(jnp.concatenate([conductance, plate_level]), (0, plates - 2 * OWNED))
    packed = jnp.concatenate([inlet_index[0, 0].T.astype(f32), plate_order.astype(f32)[None], owned[None]])
    outer, inner = swap(own, SLAB, 1), swap(own, SLAB, 0)
    odd = lax.axis_index(SLAB) % 2 == 1
    low, high = jnp.where(odd, inner, outer), jnp.where(odd, outer, inner)

    lanes_hot, rows_hot, owner = pl.pallas_call(
        prepare_kernel,
        out_shape=(
            jax.ShapeDtypeStruct((inlets // 2, 2 * LANES, 2 * plates), jnp.bfloat16),
            jax.ShapeDtypeStruct((inlets // 2, LANES, 2 * plates), f32),
            jax.ShapeDtypeStruct((8, LANES), f32),
        ),
        in_specs=[VMEM],
        out_specs=(VMEM,) * 3,
        compiler_params=pltpu.CompilerParams(vmem_limit_bytes=8 * 1024 * 1024),
        cost_estimate=pl.CostEstimate(flops=20000000, bytes_accessed=6400000, transcendentals=0),
        name="prepare",
    )(packed)

    wide = (3 * cz, cy + 2 * HALO, nx)
    tall = (wide[0], wide[1] + 2 * HALO, nx)
    cells = cz * cy
    copies = lax.axis_size("x")
    lines = tiles // (WIDTH * PACKED)
    payload, basis = pl.pallas_call(
        basis_kernel,
        out_shape=(
            jax.ShapeDtypeStruct((copies * WIDTH * (lines + 1), LANES), f32),
            jax.ShapeDtypeStruct(((DEGREE + 1) * cells, nx), f32),
        ),
        in_specs=[VMEM] * 5,
        out_specs=(VMEM, VMEM),
        scratch_shapes=[
            pltpu.VMEM(wide, f32),
            pltpu.VMEM(wide, f32),
            pltpu.VMEM(tall, f32),
            pltpu.VMEM(tall, f32),
            pltpu.VMEM((24 * 8, nx), f32),
            pltpu.VMEM((FIELDS * cells, 2 * nx), jnp.bfloat16),
            pltpu.VMEM((plates, LANES), f32),
        ],
        compiler_params=pltpu.CompilerParams(vmem_limit_bytes=8 * 1024 * 1024),
        name="basis",
    )(own, low, high, lanes_hot, rows_hot)

    group = copies * WIDTH
    arrived = lax.all_to_all(
        payload.reshape(group * (lines + 1), 1, LANES), ("x", "y"), 0, 0, tiled=True
    )
    ends = lax.axis_size("core") * lax.axis_size("z")
    rows = pl.pallas_call(
        functools.partial(rows_kernel, lines=lines),
        out_shape=jax.ShapeDtypeStruct((ends, LANES), f32),
        in_specs=[VMEM],
        out_specs=VMEM,
        compiler_params=pltpu.CompilerParams(vmem_limit_bytes=2 * 1024 * 1024),
        name="rows",
    )(arrived.reshape(group * (lines + 1), LANES))
    arrived = lax.all_to_all(rows.reshape(ends, 1, LANES), ("core", "z"), 0, 0, tiled=True)
    scale = float(1.0 / (devices * inlets) ** 0.5)
    solution, residual, flow = pl.pallas_call(
        functools.partial(final_kernel, scale=scale),
        out_shape=(
            jax.ShapeDtypeStruct((cells, nx), f32),
            jax.ShapeDtypeStruct((cells, nx), f32),
            jax.ShapeDtypeStruct((OWNED,), f32),
        ),
        in_specs=[VMEM, VMEM, VMEM],
        out_specs=(VMEM, VMEM, SMEM),
        compiler_params=pltpu.CompilerParams(vmem_limit_bytes=4 * 1024 * 1024),
        name="final",
    )(arrived.reshape(ends, LANES), basis, owner)
    return (solution.reshape(cz, cy, nx), residual.reshape(cz, cy, nx), flow)


def solution(mesh):
    slabs, tiles = mesh.devices.shape
    chips = mesh.devices.reshape(slabs // 2, 2, tiles // WIDTH, WIDTH)
    fine = jax.sharding.Mesh(chips, SLAB + TILE)
    in_specs = (
        P(SLAB, TILE, None),
        P(SLAB, TILE, None),
        P(SLAB, TILE, None, None),
        P(),
        P(TILE),
        P(TILE),
    )
    out_specs = (P(SLAB, TILE, None), P(SLAB, TILE, None), P(TILE))
    return jax.shard_map(
        on_device, mesh=fine, in_specs=in_specs, out_specs=out_specs, check_vma=False
    )
```
